512 devices in a mesh: tile: 64 (over y_hi, x, z), win: 8 (over y_lo, core).
Axes of the slice: x: 4, y: 8 (y_hi: 2, y_lo: 4; y = y_hi * 4 + y_lo), z: 8, core: 2. Of those that a mesh axis runs over, the one named last changes fastest.
Arguments:
- syndromes: int32 [32, 256, 128], P('win', 'tile'), may hold values 0 or 1
- confidence: float32 [32, 256, 128], P('win', 'tile'), may hold values from 0.25 to 2
- embed_gain: float32 [64], replicated, may hold values from -4 to 4
- embed_bias: float32 [64], replicated, may hold values from -3 to 3
- depth_kernel: float32 [4, 64, 27], replicated, may hold values from -2 to 2
- point_weight: bfloat16 [4, 64, 64], replicated, may hold values from -0.75 to 0.75
- point_bias: float32 [4, 64], replicated, may hold values from -3 to 3
- read_weight: bfloat16 [64], replicated, may hold values from -0.375 to 0.375
Outputs:
- logits: float32 [8, 16, 256, 128], P('win', None, 'tile')
The draws below stay inside these ranges and needn't reach their ends.
All inputs are finite; a program needn't handle non-finite values. No bound on the sum of `syndromes` on one device may be relied on, other than what follows from the above.
Results may differ from the reference program's by a relative error of at most 0.017.
Values may be sent and summed in bfloat16 or wider, within the bound.
A program may use at most 64 MiB of HBM per device.

```python
import math
import jax
import jax.numpy as jnp
from jax import lax

CH = 64
WINDOW = 16
COMMIT = 2
LAYERS = 4
PLANE_COLS = 128
HIST = 32
ROWS = 256
N_WIN = 8


def draw_depth_kernel(key, part):
    tap_ids = jnp.arange(27, dtype=jnp.int32)
    row_offset = tap_ids // 3 % 3
    scales = jnp.where(row_offset == 1, 0.3, 0.5).astype(jnp.float32)
    values = jax.random.normal(key, (LAYERS, CH, 27), jnp.float32)
    return jnp.clip(values * scales[None, None, :], -2.0, 2.0)


def place_ends(drawn, key, smallest, largest):
    spot = [jax.random.randint(jax.random.fold_in(key, axis), (), 0, length) for axis, length in enumerate(drawn.shape)]
    longest = drawn.shape.index(max(drawn.shape))
    next_to = spot[:longest] + [(spot[longest] + 1) % drawn.shape[longest]] + spot[longest + 1:]
    return drawn.at[tuple(spot)].set(smallest).at[tuple(next_to)].set(largest)


def levels(key, shape, shards, least, largest):
    loudness = 1.0
    for dim, shards_of in shards:
        steps = jax.random.uniform(jax.random.fold_in(jax.random.fold_in(key, 6), dim), (shards_of,), jnp.float32, least / len(shards), largest / len(shards))
        loudness = loudness * jnp.repeat(jnp.exp(steps), shape[dim] // shards_of).reshape((-1,) + (1,) * (len(shape) - 1 - dim))
    return loudness


def normal_values(rng, extent, scale, most, kind=jnp.bfloat16):
    return jnp.clip(scale * jax.random.normal(rng, extent, jnp.float32), -most, most).astype(kind)


def setup_inputs(seed: int = 0) -> dict:
    arg_keys = jax.random.split(jax.random.key(seed), 9)
    syndromes = place_ends((jax.random.randint(arg_keys[0], (HIST, ROWS, PLANE_COLS), 0, 4) < 1).astype(jnp.int32), jax.random.fold_in(arg_keys[0], 1), 0, 1)
    confidence = jnp.clip(jnp.exp(math.log(2.0) - 2.0794415 * jax.random.uniform(arg_keys[1], (HIST, ROWS, PLANE_COLS), jnp.float32) ** levels(arg_keys[1], (HIST, ROWS, PLANE_COLS), ((0, 8), (1, 64)), -0.2, 0.2)), 0.25, 2.0)
    embed_gain = normal_values(arg_keys[2], (CH,), 1.0, 4.0, jnp.float32)
    embed_bias = normal_values(arg_keys[3], (CH,), 0.5, 3.0, jnp.float32)
    depth_kernel = draw_depth_kernel(jax.random.fold_in(arg_keys[8], 71), 0)
    point_weight = normal_values(arg_keys[5], (LAYERS, CH, CH), CH ** -0.5, 0.75)
    point_bias = normal_values(arg_keys[6], (LAYERS, CH), 0.5, 3.0, jnp.float32)
    read_weight = normal_values(arg_keys[7], (CH,), (4 * CH) ** -0.5, 0.375)
    return {"syndromes": syndromes, "confidence": confidence, "embed_gain": embed_gain, "embed_bias": embed_bias, "depth_kernel": depth_kernel, "point_weight": point_weight, "point_bias": point_bias, "read_weight": read_weight}


def depthwise(features, kernel):
    padded = jnp.pad(features, ((0, 0), (1, 1), (1, 1), (1, 1)))
    rounds, rows_out, columns = features.shape[1], features.shape[2], features.shape[3]
    running = jnp.zeros(features.shape, jnp.float32)
    for offset_t in range(3):
        for offset_r in range(3):
            for offset_c in range(3):
                tap_weight = kernel[:, 9 * offset_t + 3 * offset_r + offset_c][:, None, None, None]
                part_view = padded[:, offset_t:offset_t + rounds, offset_r:offset_r + rows_out, offset_c:offset_c + columns]
                running = running + tap_weight * part_view.astype(jnp.float32)
    return running


def reference(syndromes, confidence, embed_gain, embed_bias, depth_kernel, point_weight, point_bias, read_weight):
    signed = ((2 * syndromes - 1).astype(jnp.float32) * confidence).astype(jnp.bfloat16)
    starts = jnp.arange(N_WIN, dtype=jnp.int32) * COMMIT

    def one_window(first_round):
        window = lax.dynamic_slice_in_dim(signed, first_round.astype(jnp.int32), WINDOW, 0)
        features = (window.astype(jnp.float32)[None] * embed_gain[:, None, None, None] + embed_bias[:, None, None, None]).astype(jnp.bfloat16)
        for layer_index in range(LAYERS):
            depth_out = depthwise(features, depth_kernel[layer_index]).astype(jnp.bfloat16)
            pointwise = jnp.einsum('ctrq,cd->dtrq', depth_out.astype(jnp.float32), point_weight[layer_index].astype(jnp.float32), precision=lax.Precision.HIGHEST)
            activated = jax.nn.gelu(pointwise + point_bias[layer_index][:, None, None, None], approximate=True)
            features = (features.astype(jnp.float32) + activated).astype(jnp.bfloat16)
        return jnp.einsum('ctrq,c->trq', features.astype(jnp.float32), read_weight.astype(jnp.float32), precision=lax.Precision.HIGHEST)

    return lax.map(one_window, starts)
```

```python
import jax
import jax.numpy as jnp
from jax import lax
from jax.sharding import PartitionSpec as P

WINDOW = 16
COMMIT = 2


def assemble(signed_slab, window_len):
    collected = lax.all_gather(signed_slab, "win", axis=0, tiled=True)
    first_round = lax.axis_index("win") * COMMIT
    return lax.dynamic_slice_in_dim(collected, first_round, window_len, 0)


def with_halo(block, halo):
    count = lax.axis_size("tile")
    rows = block.shape[1]
    forward = [(i, i + 1) for i in range(count - 1)]
    backward = [(i + 1, i) for i in range(count - 1)]
    low = lax.ppermute(block[:, rows - halo :], "tile", forward)
    high = lax.ppermute(block[:, :halo], "tile", backward)
    return jnp.concatenate([low, block, high], axis=1)


def depthwise(features, kernel):
    rows_in, rounds, channels, columns = features.shape
    rows_out = rows_in - 2
    padded = jnp.pad(features, ((0, 0), (1, 1), (0, 0), (1, 1)))
    running = jnp.zeros((rows_out, rounds, channels, columns), jnp.float32)
    for offset_t in range(3):
        for offset_r in range(3):
            for offset_c in range(3):
                tap_weight = kernel[:, 9 * offset_t + 3 * offset_r + offset_c][None, None, :, None]
                part_view = padded[
                    offset_r : offset_r + rows_out,
                    offset_t : offset_t + rounds,
                    :,
                    offset_c : offset_c + columns,
                ]
                running = running + tap_weight * part_view.astype(jnp.float32)
    return running


def shards(
    syndromes,
    confidence,
    embed_gain,
    embed_bias,
    depth_kernel,
    point_weight,
    point_bias,
    read_weight,
):
    layers = depth_kernel.shape[0]
    rows = syndromes.shape[1]
    signed_slab = ((2 * syndromes - 1).astype(jnp.float32) * confidence).astype(jnp.bfloat16)
    window = assemble(signed_slab, WINDOW)
    extended = with_halo(window, layers)
    first_row = lax.axis_index("tile") * rows - layers
    row_ids = first_row + jnp.arange(rows + 2 * layers)
    inside = (row_ids >= 0) & (row_ids < rows * lax.axis_size("tile"))
    planes = jnp.transpose(extended, (1, 0, 2)).astype(jnp.float32)
    features = (
        planes[:, :, None, :] * embed_gain[None, None, :, None] + embed_bias[None, None, :, None]
    ).astype(jnp.bfloat16)
    features = jnp.where(inside[:, None, None, None], features, 0).astype(jnp.bfloat16)
    for layer_index in range(layers):
        depth_out = depthwise(features, depth_kernel[layer_index]).astype(jnp.bfloat16)
        pointwise = jnp.einsum(
            "rtcq,cd->rtdq", depth_out, point_weight[layer_index], preferred_element_type=jnp.float32
        )
        activated = jax.nn.gelu(
            pointwise + point_bias[layer_index][None, None, :, None], approximate=True
        )
        features = (features[1:-1].astype(jnp.float32) + activated).astype(jnp.bfloat16)
        keep = inside[layer_index + 1 : layer_index + 1 + features.shape[0]]
        features = jnp.where(keep[:, None, None, None], features, 0).astype(jnp.bfloat16)
    logits = jnp.einsum("rtcq,c->trq", features, read_weight, preferred_element_type=jnp.float32)
    return logits[None]


def solution(mesh):
    placed = (P("win", "tile", None), P("win", "tile", None), P(), P(), P(), P(), P(), P())
    return jax.shard_map(
        shards, mesh=mesh, in_specs=placed, out_specs=P("win", None, "tile", None), check_vma=False
    )
```

```python
import functools

import jax
import jax.numpy as jnp
from jax import lax
from jax.experimental import pallas as pl
from jax.experimental.pallas import tpu as pltpu
from jax.sharding import PartitionSpec as P

WINDOW = 16
COMMIT = 2


def exchange_kernel(axis_names, halo, slab_ref, out_ref, held, recv_sem, send_sem, local_sem):
    tiles, wins = lax.axis_size("tile"), lax.axis_size("win")
    tile, win = lax.axis_index("tile"), lax.axis_index("win")
    pieces, rows = slab_ref.shape[0], slab_ref.shape[1]
    span = held.shape[0]

    def device(tile_index, win_index):
        place = {"tile": tile_index, "win": win_index}
        return tuple(place[name] for name in axis_names)

    mesh_ids = pl.DeviceIdType.MESH
    blank = jnp.zeros((span, halo) + held.shape[2:], held.dtype)

    @pl.when(tile == 0)
    def _():
        held[:, pl.ds(0, halo)] = blank

    @pl.when(tile == tiles - 1)
    def _():
        held[:, pl.ds(rows + halo, halo)] = blank

    neighbour_tiles = 1 + (tile > 0).astype(jnp.int32) + (tile < tiles - 1).astype(jnp.int32)
    barrier = pltpu.get_barrier_semaphore()
    for shift in (-1, 0, 1):
        for other in range(wins):
            there = tile + shift
            partner = (there >= 0) & (there < tiles)
            if shift == 0:
                partner = partner & (win != other)

            @pl.when(partner)
            def _():
                pl.semaphore_signal(barrier, 1, device_id=device(there, other), device_id_type=mesh_ids)

    pl.semaphore_wait(barrier, neighbour_tiles * wins - 1)

    parts = ((-1, 0, rows + halo, halo, 0), (0, 0, halo, rows, 1), (1, rows - halo, 0, halo, 0))
    started = []
    for piece in range(pieces):
        global_piece = win * pieces + piece
        for other in range(wins):
            offset = global_piece - other
            needed = (offset >= 0) & (offset < span)
            offset = jnp.clip(offset, 0, span - 1)
            for shift, src_row, dst_row, count, kind in parts:
                there = tile + shift
                ok = needed & (there >= 0) & (there < tiles)
                there = jnp.clip(there, 0, tiles - 1)
                src = slab_ref.at[pl.ds(piece, 1), pl.ds(src_row, count)]
                dst = held.at[pl.ds(offset, 1), pl.ds(dst_row, count)]
                if shift == 0:
                    local = ok & (win == other)
                    remote = ok & (win != other)
                    copy_local = pltpu.make_async_copy(src, dst, local_sem)

                    @pl.when(local)
                    def _():
                        copy_local.start()
                        copy_local.wait()
                else:
                    remote = ok
                copy = pltpu.make_async_remote_copy(
                    src_ref=src,
                    dst_ref=dst,
                    send_sem=send_sem.at[piece, other, shift + 1],
                    recv_sem=recv_sem.at[offset, shift + 1],
                    device_id=device(there, other),
                    device_id_type=mesh_ids,
                )

                @pl.when(remote)
                def _():
                    copy.start()

                started.append((remote, copy))

    for remote, copy in started:

        @pl.when(remote)
        def _():
            copy.wait_send()

    for step in range(span):
        source_win = (win + step) // pieces
        for shift, src_row, dst_row, count, kind in parts:
            there = tile - shift
            ok = (there >= 0) & (there < tiles)
            if shift == 0:
                ok = ok & (source_win != win)
            probe = pltpu.make_async_remote_copy(
                src_ref=slab_ref.at[pl.ds(0, 1), pl.ds(src_row, count)],
                dst_ref=held.at[pl.ds(0, 1), pl.ds(dst_row, count)],
                send_sem=send_sem.at[0, 0, shift + 1],
                recv_sem=recv_sem.at[step, shift + 1],
                device_id=device(there, win),
                device_id_type=mesh_ids,
            )

            @pl.when(ok)
            def _():
                probe.wait_recv()

    out_ref[...] = held[...]


def gather_window(signed_slab, halo, axis_names):
    rounds, rows, columns = signed_slab.shape
    pieces = rounds // COMMIT
    span = WINDOW // COMMIT
    cut = jnp.transpose(signed_slab.reshape(pieces, COMMIT, rows, columns), (0, 2, 1, 3))
    shape = (span, rows + 2 * halo, COMMIT, columns)
    held = pl.pallas_call(
        functools.partial(exchange_kernel, axis_names, halo),
        out_shape=jax.ShapeDtypeStruct(shape, signed_slab.dtype),
        in_specs=[pl.BlockSpec(memory_space=pltpu.VMEM)],
        out_specs=pl.BlockSpec(memory_space=pltpu.VMEM),
        scratch_shapes=[
            pltpu.VMEM(shape, signed_slab.dtype),
            pltpu.SemaphoreType.DMA((span, 3)),
            pltpu.SemaphoreType.DMA((pieces, lax.axis_size("win"), 3)),
            pltpu.SemaphoreType.DMA,
        ],
        compiler_params=pltpu.CompilerParams(collective_id=0, has_side_effects=True),
    )(cut)
    return jnp.transpose(held, (1, 0, 2, 3)).reshape(rows + 2 * halo, WINDOW, columns)


def depthwise(features, kernel):
    rows_in, rounds, channels, columns = features.shape
    rows_out = rows_in - 2
    padded = jnp.pad(features, ((0, 0), (1, 1), (0, 0), (1, 1)))
    running = jnp.zeros((rows_out, rounds, channels, columns), jnp.float32)
    for offset_t in range(3):
        for offset_r in range(3):
            for offset_c in range(3):
                tap_weight = kernel[:, 9 * offset_t + 3 * offset_r + offset_c][None, None, :, None]
                part_view = padded[
                    offset_r : offset_r + rows_out,
                    offset_t : offset_t + rounds,
                    :,
                    offset_c : offset_c + columns,
                ]
                running = running + tap_weight * part_view.astype(jnp.float32)
    return running


def shards(
    axis_names,
    syndromes,
    confidence,
    embed_gain,
    embed_bias,
    depth_kernel,
    point_weight,
    point_bias,
    read_weight,
):
    layers = depth_kernel.shape[0]
    rows = syndromes.shape[1]
    signed_slab = ((2 * syndromes - 1).astype(jnp.float32) * confidence).astype(jnp.bfloat16)
    planes = gather_window(signed_slab, layers, axis_names).astype(jnp.float32)
    first_row = lax.axis_index("tile") * rows - layers
    row_ids = first_row + jnp.arange(rows + 2 * layers)
    inside = (row_ids >= 0) & (row_ids < rows * lax.axis_size("tile"))
    features = (
        planes[:, :, None, :] * embed_gain[None, None, :, None] + embed_bias[None, None, :, None]
    ).astype(jnp.bfloat16)
    features = jnp.where(inside[:, None, None, None], features, 0).astype(jnp.bfloat16)
    for layer_index in range(layers):
        depth_out = depthwise(features, depth_kernel[layer_index]).astype(jnp.bfloat16)
        pointwise = jnp.einsum(
            "rtcq,cd->rtdq", depth_out, point_weight[layer_index], preferred_element_type=jnp.float32
        )
        activated = jax.nn.gelu(
            pointwise + point_bias[layer_index][None, None, :, None], approximate=True
        )
        features = (features[1:-1].astype(jnp.float32) + activated).astype(jnp.bfloat16)
        keep = inside[layer_index + 1 : layer_index + 1 + features.shape[0]]
        features = jnp.where(keep[:, None, None, None], features, 0).astype(jnp.bfloat16)
    logits = jnp.einsum("rtcq,c->trq", features, read_weight, preferred_element_type=jnp.float32)
    return logits[None]


def solution(mesh):
    placed = (P("win", "tile", None), P("win", "tile", None), P(), P(), P(), P(), P(), P())
    return jax.shard_map(
        functools.partial(shards, tuple(mesh.axis_names)), mesh=mesh, in_specs=placed, out_specs=P("win", None, "tile", None), check_vma=False
    )
```

```python
import functools

import jax
import jax.numpy as jnp
from jax import lax
from jax.experimental import pallas as pl
from jax.experimental.pallas import tpu as pltpu
from jax.sharding import PartitionSpec as P

WINDOW = 16
COMMIT = 2


def exchange_kernel(axis_names, halo, slab_ref, out_ref, held, recv_sem, send_sem, local_sem):
    tiles, wins = lax.axis_size("tile"), lax.axis_size("win")
    tile, win = lax.axis_index("tile"), lax.axis_index("win")
    pieces, rows = slab_ref.shape[0], slab_ref.shape[1]
    span = held.shape[0]

    def device(tile_index, win_index):
        place = {"tile": tile_index, "win": win_index}
        return tuple(place[name] for name in axis_names)

    mesh_ids = pl.DeviceIdType.MESH
    blank = jnp.zeros((span, halo) + held.shape[2:], held.dtype)

    @pl.when(tile == 0)
    def _():
        held[:, pl.ds(0, halo)] = blank

    @pl.when(tile == tiles - 1)
    def _():
        held[:, pl.ds(rows + halo, halo)] = blank

    neighbour_tiles = 1 + (tile > 0).astype(jnp.int32) + (tile < tiles - 1).astype(jnp.int32)
    barrier = pltpu.get_barrier_semaphore()
    for shift in (-1, 0, 1):
        for other in range(wins):
            there = tile + shift
            partner = (there >= 0) & (there < tiles)
            if shift == 0:
                partner = partner & (win != other)

            @pl.when(partner)
            def _():
                pl.semaphore_signal(barrier, 1, device_id=device(there, other), device_id_type=mesh_ids)

    pl.semaphore_wait(barrier, neighbour_tiles * wins - 1)

    parts = ((-1, 0, rows + halo, halo, 0), (0, 0, halo, rows, 1), (1, rows - halo, 0, halo, 0))
    started = []
    for piece in range(pieces):
        global_piece = win * pieces + piece
        for other in range(wins):
            offset = global_piece - other
            needed = (offset >= 0) & (offset < span)
            offset = jnp.clip(offset, 0, span - 1)
            for shift, src_row, dst_row, count, kind in parts:
                there = tile + shift
                ok = needed & (there >= 0) & (there < tiles)
                there = jnp.clip(there, 0, tiles - 1)
                src = slab_ref.at[pl.ds(piece, 1), pl.ds(src_row, count)]
                dst = held.at[pl.ds(offset, 1), pl.ds(dst_row, count)]
                if shift == 0:
                    local = ok & (win == other)
                    remote = ok & (win != other)
                    copy_local = pltpu.make_async_copy(src, dst, local_sem)

                    @pl.when(local)
                    def _():
                        copy_local.start()
                        copy_local.wait()
                else:
                    remote = ok
                copy = pltpu.make_async_remote_copy(
                    src_ref=src,
                    dst_ref=dst,
                    send_sem=send_sem.at[piece, other, shift + 1],
                    recv_sem=recv_sem.at[offset, shift + 1],
                    device_id=device(there, other),
                    device_id_type=mesh_ids,
                )

                @pl.when(remote)
                def _():
                    copy.start()

                started.append((remote, copy))

    for remote, copy in started:

        @pl.when(remote)
        def _():
            copy.wait_send()

    for step in range(span):
        source_win = (win + step) // pieces
        for shift, src_row, dst_row, count, kind in parts:
            there = tile - shift
            ok = (there >= 0) & (there < tiles)
            if shift == 0:
                ok = ok & (source_win != win)
            probe = pltpu.make_async_remote_copy(
                src_ref=slab_ref.at[pl.ds(0, 1), pl.ds(src_row, count)],
                dst_ref=held.at[pl.ds(0, 1), pl.ds(dst_row, count)],
                send_sem=send_sem.at[0, 0, shift + 1],
                recv_sem=recv_sem.at[step, shift + 1],
                device_id=device(there, win),
                device_id_type=mesh_ids,
            )

            @pl.when(ok)
            def _():
                probe.wait_recv()

    out_ref[...] = held[...]


def gather_window(signed_slab, halo, axis_names):
    rounds, rows, columns = signed_slab.shape
    pieces = rounds // COMMIT
    span = WINDOW // COMMIT
    cut = jnp.transpose(signed_slab.reshape(pieces, COMMIT, rows, columns), (0, 2, 1, 3))
    shape = (span, rows + 2 * halo, COMMIT, columns)
    held = pl.pallas_call(
        functools.partial(exchange_kernel, axis_names, halo),
        out_shape=jax.ShapeDtypeStruct(shape, signed_slab.dtype),
        in_specs=[pl.BlockSpec(memory_space=pltpu.VMEM)],
        out_specs=pl.BlockSpec(memory_space=pltpu.VMEM),
        scratch_shapes=[
            pltpu.VMEM(shape, signed_slab.dtype),
            pltpu.SemaphoreType.DMA((span, 3)),
            pltpu.SemaphoreType.DMA((pieces, lax.axis_size("win"), 3)),
            pltpu.SemaphoreType.DMA,
        ],
        compiler_params=pltpu.CompilerParams(collective_id=0, has_side_effects=True),
    )(cut)
    return jnp.transpose(held, (1, 0, 2, 3)).reshape(rows + 2 * halo, WINDOW, columns)


def gelu(value):
    return 0.5 * value * (1.0 + jnp.tanh(0.7978845608028654 * (value + 0.044715 * (value * value * value))))


def network_kernel(
    rows, halo, planes_ref, gain_ref, bias_ref, taps_ref, mix_ref, shift_ref, read_ref,
    out_ref, feats, depth,
):
    layers = taps_ref.shape[0]
    extended, rounds, columns = planes_ref.shape
    channels = gain_ref.shape[0]
    groups = channels // 8
    tiles = lax.axis_size("tile")
    first_row = lax.axis_index("tile") * rows - halo

    def inside(row):
        plane_row = first_row + row
        return (plane_row >= 0) & (plane_row < rows * tiles)

    def embed(row, carry):
        keep = inside(row)
        for t in range(rounds):
            value = planes_ref[row, pl.ds(t, 1), :] * gain_ref[...] + bias_ref[...]
            value = value.astype(jnp.bfloat16).astype(jnp.float32)
            feats[0, row, :, pl.ds(t * columns, columns)] = jnp.where(keep, value, 0.0)
        return carry

    lax.fori_loop(0, extended, embed, 0)
    lane = lax.broadcasted_iota(jnp.int32, (8, columns), 1)

    def spread(value):
        left = jnp.where(lane == 0, 0.0, pltpu.roll(value, 1, 1))
        right = jnp.where(lane == columns - 1, 0.0, pltpu.roll(value, columns - 1, 1))
        return (left, value, right)

    for layer in range(layers):
        src, dst = layer % 2, (layer + 1) % 2
        last = layer == layers - 1

        def one_row(row, carry, layer=layer, src=src, dst=dst, last=last):
            def one_group(group, inner):
                lanes8 = pl.ds(pl.multiple_of(group * 8, 8), 8)
                weights = [taps_ref[layer, tap, lanes8, :] for tap in range(27)]
                window = {}

                def load(t):
                    if t < 0 or t >= rounds:
                        return None
                    return [spread(feats[src, row - 1 + b, lanes8, pl.ds(t * columns, columns)]) for b in range(3)]

                window[-1] = None
                window[0] = load(0)
                for t in range(rounds):
                    window[t + 1] = load(t + 1)
                    total = None
                    for a in range(3):
                        held = window[t + a - 1]
                        if held is None:
                            continue
                        for b in range(3):
                            for e in range(3):
                                term = weights[9 * a + 3 * b + e] * held[b][e]
                                total = term if total is None else total + term
                    depth[lanes8, pl.ds(t * columns, columns)] = total
                    window.pop(t - 1, None)
                return inner

            lax.fori_loop(0, groups, one_group, 0)
            mixed = jnp.dot(
                mix_ref[layer], depth[...].astype(jnp.bfloat16), preferred_element_type=jnp.float32
            )
            keep = inside(row)
            sums = []
            for t in range(rounds):
                cut = pl.ds(t * columns, columns)
                activated = gelu(mixed[:, t * columns : (t + 1) * columns] + shift_ref[layer])
                value = (feats[src, row, :, cut] + activated).astype(jnp.bfloat16).astype(jnp.float32)
                value = jnp.where(keep, value, 0.0)
                if last:
                    sums.append(jnp.sum(value * read_ref[...], axis=0, keepdims=True))
                else:
                    feats[dst, row, :, cut] = value
            if last:
                out_ref[row - halo] = jnp.concatenate(sums, axis=0)
            return carry

        lax.fori_loop(layer + 1, extended - layer - 1, one_row, 0)


def run_network(planes, embed_gain, embed_bias, depth_kernel, point_weight, point_bias, read_weight, rows, halo):
    extended, rounds, columns = planes.shape
    layers, channels, _ = depth_kernel.shape
    wide = lambda v: jnp.broadcast_to(v.astype(jnp.float32)[..., None], v.shape + (columns,))
    taps = wide(jnp.transpose(depth_kernel, (0, 2, 1)))
    mix = jnp.transpose(point_weight, (0, 2, 1)).astype(jnp.bfloat16)
    vmem = pl.BlockSpec(memory_space=pltpu.VMEM)
    return pl.pallas_call(
        functools.partial(network_kernel, rows, halo),
        out_shape=jax.ShapeDtypeStruct((rows, rounds, columns), jnp.float32),
        in_specs=[vmem] * 7,
        out_specs=vmem,
        scratch_shapes=[
            pltpu.VMEM((2, extended, channels, rounds * columns), jnp.float32),
            pltpu.VMEM((channels, rounds * columns), jnp.float32),
        ],
        compiler_params=pltpu.CompilerParams(vmem_limit_bytes=56 * 1024 * 1024),
    )(planes, wide(embed_gain), wide(embed_bias), taps, mix, wide(point_bias), wide(read_weight))


def shards(
    axis_names,
    syndromes,
    confidence,
    embed_gain,
    embed_bias,
    depth_kernel,
    point_weight,
    point_bias,
    read_weight,
):
    layers = depth_kernel.shape[0]
    rows = syndromes.shape[1]
    signed_slab = ((2 * syndromes - 1).astype(jnp.float32) * confidence).astype(jnp.bfloat16)
    planes = gather_window(signed_slab, layers, axis_names).astype(jnp.float32)
    logits = run_network(
        planes, embed_gain, embed_bias, depth_kernel, point_weight, point_bias, read_weight, rows, layers
    )
    return jnp.transpose(logits, (1, 0, 2))[None]


def solution(mesh):
    placed = (P("win", "tile", None), P("win", "tile", None), P(), P(), P(), P(), P(), P())
    return jax.shard_map(
        functools.partial(shards, tuple(mesh.axis_names)), mesh=mesh, in_specs=placed, out_specs=P("win", None, "tile", None), check_vma=False
    )
```

```python
import functools

import jax
import jax.numpy as jnp
from jax import lax
from jax.experimental import pallas as pl
from jax.experimental.pallas import tpu as pltpu
from jax.sharding import PartitionSpec as P

WINDOW = 16
COMMIT = 2


def exchange_kernel(axis_names, halo, slab_ref, out_ref, held, recv_sem, send_sem, local_sem):
    tiles, wins = lax.axis_size("tile"), lax.axis_size("win")
    tile, win = lax.axis_index("tile"), lax.axis_index("win")
    pieces, rows = slab_ref.shape[0], slab_ref.shape[1]
    span = held.shape[0]

    def device(tile_index, win_index):
        place = {"tile": tile_index, "win": win_index}
        return tuple(place[name] for name in axis_names)

    mesh_ids = pl.DeviceIdType.MESH
    blank = jnp.zeros((span, halo) + held.shape[2:], held.dtype)

    @pl.when(tile == 0)
    def _():
        held[:, pl.ds(0, halo)] = blank

    @pl.when(tile == tiles - 1)
    def _():
        held[:, pl.ds(rows + halo, halo)] = blank

    neighbour_tiles = 1 + (tile > 0).astype(jnp.int32) + (tile < tiles - 1).astype(jnp.int32)
    barrier = pltpu.get_barrier_semaphore()
    for shift in (-1, 0, 1):
        for other in range(wins):
            there = tile + shift
            partner = (there >= 0) & (there < tiles)
            if shift == 0:
                partner = partner & (win != other)

            @pl.when(partner)
            def _():
                pl.semaphore_signal(barrier, 1, device_id=device(there, other), device_id_type=mesh_ids)

    pl.semaphore_wait(barrier, neighbour_tiles * wins - 1)

    parts = ((-1, 0, rows + halo, halo, 0), (0, 0, halo, rows, 1), (1, rows - halo, 0, halo, 0))
    started = []
    for piece in range(pieces):
        global_piece = win * pieces + piece
        for other in range(wins):
            offset = global_piece - other
            needed = (offset >= 0) & (offset < span)
            offset = jnp.clip(offset, 0, span - 1)
            for shift, src_row, dst_row, count, kind in parts:
                there = tile + shift
                ok = needed & (there >= 0) & (there < tiles)
                there = jnp.clip(there, 0, tiles - 1)
                src = slab_ref.at[pl.ds(piece, 1), pl.ds(src_row, count)]
                dst = held.at[pl.ds(offset, 1), pl.ds(dst_row, count)]
                if shift == 0:
                    local = ok & (win == other)
                    remote = ok & (win != other)
                    copy_local = pltpu.make_async_copy(src, dst, local_sem)

                    @pl.when(local)
                    def _():
                        copy_local.start()
                        copy_local.wait()
                else:
                    remote = ok
                copy = pltpu.make_async_remote_copy(
                    src_ref=src,
                    dst_ref=dst,
                    send_sem=send_sem.at[piece, other, shift + 1],
                    recv_sem=recv_sem.at[offset, shift + 1],
                    device_id=device(there, other),
                    device_id_type=mesh_ids,
                )

                @pl.when(remote)
                def _():
                    copy.start()

                started.append((remote, copy))

    for remote, copy in started:

        @pl.when(remote)
        def _():
            copy.wait_send()

    for step in range(span):
        source_win = (win + step) // pieces
        for shift, src_row, dst_row, count, kind in parts:
            there = tile - shift
            ok = (there >= 0) & (there < tiles)
            if shift == 0:
                ok = ok & (source_win != win)
            probe = pltpu.make_async_remote_copy(
                src_ref=slab_ref.at[pl.ds(0, 1), pl.ds(src_row, count)],
                dst_ref=held.at[pl.ds(0, 1), pl.ds(dst_row, count)],
                send_sem=send_sem.at[0, 0, shift + 1],
                recv_sem=recv_sem.at[step, shift + 1],
                device_id=device(there, win),
                device_id_type=mesh_ids,
            )

            @pl.when(ok)
            def _():
                probe.wait_recv()

    out_ref[...] = held[...]


def gather_window(signed_slab, halo, axis_names):
    rounds, rows, columns = signed_slab.shape
    pieces = rounds // COMMIT
    span = WINDOW // COMMIT
    cut = jnp.transpose(signed_slab.reshape(pieces, COMMIT, rows, columns), (0, 2, 1, 3))
    shape = (span, rows + 2 * halo, COMMIT, columns)
    held = pl.pallas_call(
        functools.partial(exchange_kernel, axis_names, halo),
        out_shape=jax.ShapeDtypeStruct(shape, signed_slab.dtype),
        in_specs=[pl.BlockSpec(memory_space=pltpu.VMEM)],
        out_specs=pl.BlockSpec(memory_space=pltpu.VMEM),
        scratch_shapes=[
            pltpu.VMEM(shape, signed_slab.dtype),
            pltpu.SemaphoreType.DMA((span, 3)),
            pltpu.SemaphoreType.DMA((pieces, lax.axis_size("win"), 3)),
            pltpu.SemaphoreType.DMA,
        ],
        compiler_params=pltpu.CompilerParams(collective_id=0, has_side_effects=True),
    )(cut)
    return jnp.transpose(held, (1, 0, 2, 3)).reshape(rows + 2 * halo, WINDOW, columns)


def gelu(value):
    return 0.5 * value * (1.0 + jnp.tanh(0.7978845608028654 * (value + 0.044715 * (value * value * value))))


def network_kernel(rows, halo, layers, planes_ref, slabs_ref, mix_ref, out_ref, feats, depth):
    extended, rounds, columns = planes_ref.shape
    channels = slabs_ref.shape[1]
    tail = 28 * layers
    gain_ref, bias_ref, read_ref = slabs_ref.at[tail], slabs_ref.at[tail + 1], slabs_ref.at[tail + 2]
    groups = channels // 8
    tiles = lax.axis_size("tile")
    first_row = lax.axis_index("tile") * rows - halo

    def inside(row):
        plane_row = first_row + row
        return (plane_row >= 0) & (plane_row < rows * tiles)

    def embed(row, carry):
        keep = inside(row)
        for t in range(rounds):
            value = planes_ref[row, pl.ds(t, 1), :] * gain_ref[...] + bias_ref[...]
            value = value.astype(jnp.bfloat16).astype(jnp.float32)
            feats[0, row, :, pl.ds(t * columns, columns)] = jnp.where(keep, value, 0.0)
        return carry

    lax.fori_loop(0, extended, embed, 0)
    lane = lax.broadcasted_iota(jnp.int32, (8, columns), 1)

    def spread(value):
        left = jnp.where(lane == 0, 0.0, pltpu.roll(value, 1, 1))
        right = jnp.where(lane == columns - 1, 0.0, pltpu.roll(value, columns - 1, 1))
        return (left, value, right)

    for layer in range(layers):
        src, dst = layer % 2, (layer + 1) % 2
        last = layer == layers - 1

        def one_row(row, carry, layer=layer, src=src, dst=dst, last=last):
            def one_group(group, inner):
                lanes8 = pl.ds(pl.multiple_of(group * 8, 8), 8)
                weights = [slabs_ref[27 * layer + tap, lanes8, :] for tap in range(27)]
                window = {}

                def load(t):
                    if t < 0 or t >= rounds:
                        return None
                    return [spread(feats[src, row - 1 + b, lanes8, pl.ds(t * columns, columns)]) for b in range(3)]

                window[-1] = None
                window[0] = load(0)
                for t in range(rounds):
                    window[t + 1] = load(t + 1)
                    total = None
                    for a in range(3):
                        held = window[t + a - 1]
                        if held is None:
                            continue
                        for b in range(3):
                            for e in range(3):
                                term = weights[9 * a + 3 * b + e] * held[b][e]
                                total = term if total is None else total + term
                    depth[lanes8, pl.ds(t * columns, columns)] = total
                    window.pop(t - 1, None)
                return inner

            lax.fori_loop(0, groups, one_group, 0)
            mixed = jnp.dot(
                mix_ref[layer], depth[...].astype(jnp.bfloat16), preferred_element_type=jnp.float32
            )
            keep = inside(row)
            sums = []
            for t in range(rounds):
                cut = pl.ds(t * columns, columns)
                activated = gelu(mixed[:, t * columns : (t + 1) * columns] + slabs_ref[27 * layers + layer])
                value = (feats[src, row, :, cut] + activated).astype(jnp.bfloat16).astype(jnp.float32)
                value = jnp.where(keep, value, 0.0)
                if last:
                    sums.append(jnp.sum(value * read_ref[...], axis=0, keepdims=True))
                else:
                    feats[dst, row, :, cut] = value
            if last:
                out_ref[row - halo] = jnp.concatenate(sums, axis=0)
            return carry

        lax.fori_loop(layer + 1, extended - layer - 1, one_row, 0)


def run_network(planes, embed_gain, embed_bias, depth_kernel, point_weight, point_bias, read_weight, rows, halo):
    extended, rounds, columns = planes.shape
    layers, channels, _ = depth_kernel.shape
    stacked = jnp.concatenate(
        [
            jnp.transpose(depth_kernel, (0, 2, 1)).reshape(-1, channels),
            point_bias,
            embed_gain[None],
            embed_bias[None],
            read_weight.astype(jnp.float32)[None],
        ],
        axis=0,
    )
    slabs = jnp.broadcast_to(stacked[..., None], stacked.shape + (columns,))
    mix = jnp.transpose(point_weight, (0, 2, 1)).astype(jnp.bfloat16)
    vmem = pl.BlockSpec(memory_space=pltpu.VMEM)
    return pl.pallas_call(
        functools.partial(network_kernel, rows, halo, layers),
        out_shape=jax.ShapeDtypeStruct((rows, rounds, columns), jnp.float32),
        in_specs=[vmem] * 3,
        out_specs=vmem,
        scratch_shapes=[
            pltpu.VMEM((2, extended, channels, rounds * columns), jnp.float32),
            pltpu.VMEM((channels, rounds * columns), jnp.float32),
        ],
        compiler_params=pltpu.CompilerParams(vmem_limit_bytes=56 * 1024 * 1024),
    )(planes, slabs, mix)


def shards(
    axis_names,
    syndromes,
    confidence,
    embed_gain,
    embed_bias,
    depth_kernel,
    point_weight,
    point_bias,
    read_weight,
):
    layers = depth_kernel.shape[0]
    rows = syndromes.shape[1]
    signed_slab = ((2 * syndromes - 1).astype(jnp.float32) * confidence).astype(jnp.bfloat16)
    planes = gather_window(signed_slab, layers, axis_names).astype(jnp.float32)
    logits = run_network(
        planes, embed_gain, embed_bias, depth_kernel, point_weight, point_bias, read_weight, rows, layers
    )
    return jnp.transpose(logits, (1, 0, 2))[None]


def solution(mesh):
    placed = (P("win", "tile", None), P("win", "tile", None), P(), P(), P(), P(), P(), P())
    return jax.shard_map(
        functools.partial(shards, tuple(mesh.axis_names)), mesh=mesh, in_specs=placed, out_specs=P("win", None, "tile", None), check_vma=False
    )
```

```python
import functools

import jax
import jax.numpy as jnp
from jax import lax
from jax.experimental import pallas as pl
from jax.experimental.pallas import tpu as pltpu
from jax.sharding import PartitionSpec as P

WINDOW = 16
COMMIT = 2


def exchange_kernel(axis_names, halo, slab_ref, out_ref, held, recv_sem, send_sem, local_sem):
    tiles, wins = lax.axis_size("tile"), lax.axis_size("win")
    tile, win = lax.axis_index("tile"), lax.axis_index("win")
    pieces, rows = slab_ref.shape[0], slab_ref.shape[1]
    span = held.shape[0]

    def device(tile_index, win_index):
        place = {"tile": tile_index, "win": win_index}
        return tuple(place[name] for name in axis_names)

    mesh_ids = pl.DeviceIdType.MESH
    blank = jnp.zeros((span, halo) + held.shape[2:], held.dtype)

    @pl.when(tile == 0)
    def _():
        held[:, pl.ds(0, halo)] = blank

    @pl.when(tile == tiles - 1)
    def _():
        held[:, pl.ds(rows + halo, halo)] = blank

    neighbour_tiles = 1 + (tile > 0).astype(jnp.int32) + (tile < tiles - 1).astype(jnp.int32)
    barrier = pltpu.get_barrier_semaphore()
    for shift in (-1, 0, 1):
        for other in range(wins):
            there = tile + shift
            partner = (there >= 0) & (there < tiles)
            if shift == 0:
                partner = partner & (win != other)

            @pl.when(partner)
            def _():
                pl.semaphore_signal(barrier, 1, device_id=device(there, other), device_id_type=mesh_ids)

    pl.semaphore_wait(barrier, neighbour_tiles * wins - 1)

    parts = ((-1, 0, rows + halo, halo, 0), (0, 0, halo, rows, 1), (1, rows - halo, 0, halo, 0))
    started = []
    for piece in range(pieces):
        global_piece = win * pieces + piece
        for other in range(wins):
            offset = global_piece - other
            needed = (offset >= 0) & (offset < span)
            offset = jnp.clip(offset, 0, span - 1)
            for shift, src_row, dst_row, count, kind in parts:
                there = tile + shift
                ok = needed & (there >= 0) & (there < tiles)
                there = jnp.clip(there, 0, tiles - 1)
                src = slab_ref.at[pl.ds(piece, 1), pl.ds(src_row, count)]
                dst = held.at[pl.ds(offset, 1), pl.ds(dst_row, count)]
                if shift == 0:
                    local = ok & (win == other)
                    remote = ok & (win != other)
                    copy_local = pltpu.make_async_copy(src, dst, local_sem)

                    @pl.when(local)
                    def _():
                        copy_local.start()
                        copy_local.wait()
                else:
                    remote = ok
                copy = pltpu.make_async_remote_copy(
                    src_ref=src,
                    dst_ref=dst,
                    send_sem=send_sem.at[piece, other, shift + 1],
                    recv_sem=recv_sem.at[offset, shift + 1],
                    device_id=device(there, other),
                    device_id_type=mesh_ids,
                )

                @pl.when(remote)
                def _():
                    copy.start()

                started.append((remote, copy))

    for remote, copy in started:

        @pl.when(remote)
        def _():
            copy.wait_send()

    for step in range(span):
        source_win = (win + step) // pieces
        for shift, src_row, dst_row, count, kind in parts:
            there = tile - shift
            ok = (there >= 0) & (there < tiles)
            if shift == 0:
                ok = ok & (source_win != win)
            probe = pltpu.make_async_remote_copy(
                src_ref=slab_ref.at[pl.ds(0, 1), pl.ds(src_row, count)],
                dst_ref=held.at[pl.ds(0, 1), pl.ds(dst_row, count)],
                send_sem=send_sem.at[0, 0, shift + 1],
                recv_sem=recv_sem.at[step, shift + 1],
                device_id=device(there, win),
                device_id_type=mesh_ids,
            )

            @pl.when(ok)
            def _():
                probe.wait_recv()

    out_ref[...] = held[...]


def gather_window(signed_slab, halo, axis_names):
    rounds, rows, columns = signed_slab.shape
    pieces = rounds // COMMIT
    span = WINDOW // COMMIT
    cut = jnp.transpose(signed_slab.reshape(pieces, COMMIT, rows, columns), (0, 2, 1, 3))
    shape = (span, rows + 2 * halo, COMMIT, columns)
    held = pl.pallas_call(
        functools.partial(exchange_kernel, axis_names, halo),
        out_shape=jax.ShapeDtypeStruct(shape, signed_slab.dtype),
        in_specs=[pl.BlockSpec(memory_space=pltpu.VMEM)],
        out_specs=pl.BlockSpec(memory_space=pltpu.VMEM),
        scratch_shapes=[
            pltpu.VMEM(shape, signed_slab.dtype),
            pltpu.SemaphoreType.DMA((span, 3)),
            pltpu.SemaphoreType.DMA((pieces, lax.axis_size("win"), 3)),
            pltpu.SemaphoreType.DMA,
        ],
        compiler_params=pltpu.CompilerParams(collective_id=0, has_side_effects=True),
    )(cut)
    return jnp.transpose(held, (1, 0, 2, 3)).reshape(rows + 2 * halo, WINDOW, columns)


def gelu(value):
    return 0.5 * value * (1.0 + jnp.tanh(0.7978845608028654 * (value + 0.044715 * (value * value * value))))


def network_kernel(rows, halo, layers, planes_ref, slabs_ref, mix_ref, out_ref, feats, depth):
    extended, rounds, columns = planes_ref.shape
    channels = slabs_ref.shape[1]
    tail = 28 * layers
    gain_ref, bias_ref, read_ref = slabs_ref.at[tail], slabs_ref.at[tail + 1], slabs_ref.at[tail + 2]
    groups = channels // 8
    tiles = lax.axis_size("tile")
    first_row = lax.axis_index("tile") * rows - halo

    def inside(row):
        plane_row = first_row + row
        return (plane_row >= 0) & (plane_row < rows * tiles)

    def embed(row, carry):
        keep = inside(row)
        for t in range(rounds):
            value = planes_ref[row, pl.ds(t, 1), :] * gain_ref[...] + bias_ref[...]
            value = value.astype(jnp.bfloat16).astype(jnp.float32)
            feats[0, row, :, pl.ds(t * columns, columns)] = jnp.where(keep, value, 0.0)
        return carry

    lax.fori_loop(0, extended, embed, 0)

    def spread(value):
        return (pltpu.roll(value, 1, 1), value, pltpu.roll(value, columns - 1, 1))

    for layer in range(layers):
        src, dst = layer % 2, (layer + 1) % 2
        last = layer == layers - 1

        def one_row(row, carry, layer=layer, src=src, dst=dst, last=last):
            def one_group(group, inner):
                lanes8 = pl.ds(pl.multiple_of(group * 8, 8), 8)
                weights = [slabs_ref[27 * layer + tap, lanes8, :] for tap in range(27)]
                running = {}
                for source in range(rounds):
                    cut = pl.ds(source * columns, columns)
                    held = [spread(feats[src, row - 1 + b, lanes8, cut]) for b in range(3)]
                    for a in range(3):
                        t = source - a + 1
                        if t < 0 or t >= rounds:
                            continue
                        for b in range(3):
                            for e in range(3):
                                term = weights[9 * a + 3 * b + e] * held[b][e]
                                running[t] = term if t not in running else running[t] + term
                    done = source - 1 if source < rounds - 1 else None
                    for t in ([done] if done is not None else [rounds - 2, rounds - 1]):
                        if t >= 0:
                            depth[lanes8, pl.ds(t * columns, columns)] = running.pop(t)
                return inner

            lax.fori_loop(0, groups, one_group, 0, unroll=2)
            mixed = jnp.dot(
                mix_ref[layer], depth[...].astype(jnp.bfloat16), preferred_element_type=jnp.float32
            )
            keep = inside(row)
            sums = []
            for t in range(rounds):
                cut = pl.ds(t * columns, columns)
                activated = gelu(mixed[:, t * columns : (t + 1) * columns] + slabs_ref[27 * layers + layer])
                value = (feats[src, row, :, cut] + activated).astype(jnp.bfloat16).astype(jnp.float32)
                value = jnp.where(keep, value, 0.0)
                if last:
                    sums.append(jnp.sum(value * read_ref[...], axis=0, keepdims=True))
                else:
                    feats[dst, row, :, cut] = value
            if last:
                out_ref[row - halo] = jnp.concatenate(sums, axis=0)
            return carry

        lax.fori_loop(layer + 1, extended - layer - 1, one_row, 0)


def run_network(planes, embed_gain, embed_bias, depth_kernel, point_weight, point_bias, read_weight, rows, halo):
    extended, rounds, columns = planes.shape
    layers, channels, _ = depth_kernel.shape
    stacked = jnp.concatenate(
        [
            jnp.transpose(depth_kernel, (0, 2, 1)).reshape(-1, channels),
            point_bias,
            embed_gain[None],
            embed_bias[None],
            read_weight.astype(jnp.float32)[None],
        ],
        axis=0,
    )
    slabs = jnp.broadcast_to(stacked[..., None], stacked.shape + (columns,))
    lane = jnp.arange(columns)
    side = jnp.arange(stacked.shape[0]) % 3
    tap_rows = jnp.arange(stacked.shape[0]) < 27 * layers
    cancel = tap_rows[:, None] & (((side[:, None] == 0) & (lane == 0)) | ((side[:, None] == 2) & (lane == columns - 1)))
    slabs = jnp.where(cancel[:, None, :], 0.0, slabs)
    mix = jnp.transpose(point_weight, (0, 2, 1)).astype(jnp.bfloat16)
    vmem = pl.BlockSpec(memory_space=pltpu.VMEM)
    return pl.pallas_call(
        functools.partial(network_kernel, rows, halo, layers),
        out_shape=jax.ShapeDtypeStruct((rows, rounds, columns), jnp.float32),
        in_specs=[vmem] * 3,
        out_specs=vmem,
        scratch_shapes=[
            pltpu.VMEM((2, extended, channels, rounds * columns), jnp.float32),
            pltpu.VMEM((channels, rounds * columns), jnp.float32),
        ],
        compiler_params=pltpu.CompilerParams(vmem_limit_bytes=56 * 1024 * 1024),
    )(planes, slabs, mix)


def shards(
    axis_names,
    syndromes,
    confidence,
    embed_gain,
    embed_bias,
    depth_kernel,
    point_weight,
    point_bias,
    read_weight,
):
    layers = depth_kernel.shape[0]
    rows = syndromes.shape[1]
    signed_slab = ((2 * syndromes - 1).astype(jnp.float32) * confidence).astype(jnp.bfloat16)
    planes = gather_window(signed_slab, layers, axis_names).astype(jnp.float32)
    logits = run_network(
        planes, embed_gain, embed_bias, depth_kernel, point_weight, point_bias, read_weight, rows, layers
    )
    return jnp.transpose(logits, (1, 0, 2))[None]


def solution(mesh):
    placed = (P("win", "tile", None), P("win", "tile", None), P(), P(), P(), P(), P(), P())
    return jax.shard_map(
        functools.partial(shards, tuple(mesh.axis_names)), mesh=mesh, in_specs=placed, out_specs=P("win", None, "tile", None), check_vma=False
    )
```

```python
import functools

import jax
import jax.numpy as jnp
from jax import lax
from jax.experimental import pallas as pl
from jax.experimental.pallas import tpu as pltpu
from jax.sharding import PartitionSpec as P

WINDOW = 16
COMMIT = 2


def exchange_kernel(axis_names, halo, slab_ref, out_ref, held, recv_sem, send_sem, local_sem):
    tiles, wins = lax.axis_size("tile"), lax.axis_size("win")
    tile, win = lax.axis_index("tile"), lax.axis_index("win")
    pieces, rows = slab_ref.shape[0], slab_ref.shape[1]
    span = held.shape[0]

    def device(tile_index, win_index):
        place = {"tile": tile_index, "win": win_index}
        return tuple(place[name] for name in axis_names)

    mesh_ids = pl.DeviceIdType.MESH
    blank = jnp.zeros((span, halo) + held.shape[2:], held.dtype)

    @pl.when(tile == 0)
    def _():
        held[:, pl.ds(0, halo)] = blank

    @pl.when(tile == tiles - 1)
    def _():
        held[:, pl.ds(rows + halo, halo)] = blank

    neighbour_tiles = 1 + (tile > 0).astype(jnp.int32) + (tile < tiles - 1).astype(jnp.int32)
    barrier = pltpu.get_barrier_semaphore()
    for shift in (-1, 0, 1):
        for other in range(wins):
            there = tile + shift
            partner = (there >= 0) & (there < tiles)
            if shift == 0:
                partner = partner & (win != other)

            @pl.when(partner)
            def _():
                pl.semaphore_signal(barrier, 1, device_id=device(there, other), device_id_type=mesh_ids)

    pl.semaphore_wait(barrier, neighbour_tiles * wins - 1)

    parts = ((-1, 0, rows + halo, halo, 0), (0, 0, halo, rows, 1), (1, rows - halo, 0, halo, 0))
    started = []
    for piece in range(pieces):
        global_piece = win * pieces + piece
        for other in range(wins):
            offset = global_piece - other
            needed = (offset >= 0) & (offset < span)
            offset = jnp.clip(offset, 0, span - 1)
            for shift, src_row, dst_row, count, kind in parts:
                there = tile + shift
                ok = needed & (there >= 0) & (there < tiles)
                there = jnp.clip(there, 0, tiles - 1)
                src = slab_ref.at[pl.ds(piece, 1), pl.ds(src_row, count)]
                dst = held.at[pl.ds(offset, 1), pl.ds(dst_row, count)]
                if shift == 0:
                    local = ok & (win == other)
                    remote = ok & (win != other)
                    copy_local = pltpu.make_async_copy(src, dst, local_sem)

                    @pl.when(local)
                    def _():
                        copy_local.start()
                        copy_local.wait()
                else:
                    remote = ok
                copy = pltpu.make_async_remote_copy(
                    src_ref=src,
                    dst_ref=dst,
                    send_sem=send_sem.at[piece, other, shift + 1],
                    recv_sem=recv_sem.at[offset, shift + 1],
                    device_id=device(there, other),
                    device_id_type=mesh_ids,
                )

                @pl.when(remote)
                def _():
                    copy.start()

                started.append((remote, copy))

    for remote, copy in started:

        @pl.when(remote)
        def _():
            copy.wait_send()

    for step in range(span):
        source_win = (win + step) // pieces
        for shift, src_row, dst_row, count, kind in parts:
            there = tile - shift
            ok = (there >= 0) & (there < tiles)
            if shift == 0:
                ok = ok & (source_win != win)
            probe = pltpu.make_async_remote_copy(
                src_ref=slab_ref.at[pl.ds(0, 1), pl.ds(src_row, count)],
                dst_ref=held.at[pl.ds(0, 1), pl.ds(dst_row, count)],
                send_sem=send_sem.at[0, 0, shift + 1],
                recv_sem=recv_sem.at[step, shift + 1],
                device_id=device(there, win),
                device_id_type=mesh_ids,
            )

            @pl.when(ok)
            def _():
                probe.wait_recv()

    out_ref[...] = held[...]


def gather_window(signed_slab, halo, axis_names):
    rounds, rows, columns = signed_slab.shape
    pieces = rounds // COMMIT
    span = WINDOW // COMMIT
    cut = jnp.transpose(signed_slab.reshape(pieces, COMMIT, rows, columns), (0, 2, 1, 3))
    shape = (span, rows + 2 * halo, COMMIT, columns)
    held = pl.pallas_call(
        functools.partial(exchange_kernel, axis_names, halo),
        out_shape=jax.ShapeDtypeStruct(shape, signed_slab.dtype),
        in_specs=[pl.BlockSpec(memory_space=pltpu.VMEM)],
        out_specs=pl.BlockSpec(memory_space=pltpu.VMEM),
        scratch_shapes=[
            pltpu.VMEM(shape, signed_slab.dtype),
            pltpu.SemaphoreType.DMA((span, 3)),
            pltpu.SemaphoreType.DMA((pieces, lax.axis_size("win"), 3)),
            pltpu.SemaphoreType.DMA,
        ],
        compiler_params=pltpu.CompilerParams(collective_id=0, has_side_effects=True),
    )(cut)
    return jnp.transpose(held, (1, 0, 2, 3)).reshape(rows + 2 * halo, WINDOW, columns)


def gelu(value):
    return 0.5 * value * (1.0 + jnp.tanh(0.7978845608028654 * (value + 0.044715 * (value * value * value))))


def network_kernel(rows, halo, layers, planes_ref, slabs_ref, mix_ref, out_ref, feats, depth):
    extended, rounds, columns = planes_ref.shape
    channels = slabs_ref.shape[1]
    tail = 28 * layers
    gain_ref, bias_ref, read_ref = slabs_ref.at[tail], slabs_ref.at[tail + 1], slabs_ref.at[tail + 2]
    groups = channels // 8
    tiles = lax.axis_size("tile")
    first_row = lax.axis_index("tile") * rows - halo

    def inside(row):
        plane_row = first_row + row
        return (plane_row >= 0) & (plane_row < rows * tiles)

    def embed(row, carry):
        keep = inside(row)
        for t in range(rounds):
            value = planes_ref[row, pl.ds(t, 1), :] * gain_ref[...] + bias_ref[...]
            value = value.astype(jnp.bfloat16).astype(jnp.float32)
            feats[0, row, :, pl.ds(t * columns, columns)] = jnp.where(keep, value, 0.0)
        return carry

    lax.fori_loop(0, extended, embed, 0)

    def spread(value):
        return (pltpu.roll(value, 1, 1), value, pltpu.roll(value, columns - 1, 1))

    for layer in range(layers):
        src, dst = layer % 2, (layer + 1) % 2
        last = layer == layers - 1

        def one_row(row, carry, layer=layer, src=src, dst=dst, last=last):
            def one_group(group, inner):
                lanes8 = pl.ds(pl.multiple_of(group * 8, 8), 8)
                weights = [slabs_ref[27 * layer + tap, lanes8, :] for tap in range(27)]
                running = {}
                for source in range(rounds):
                    cut = pl.ds(source * columns, columns)
                    held = [spread(feats[src, row - 1 + b, lanes8, cut]) for b in range(3)]
                    for a in range(3):
                        t = source - a + 1
                        if t < 0 or t >= rounds:
                            continue
                        for b in range(3):
                            for e in range(3):
                                term = weights[9 * a + 3 * b + e] * held[b][e]
                                running[t] = term if t not in running else running[t] + term
                    done = source - 1 if source < rounds - 1 else None
                    for t in ([done] if done is not None else [rounds - 2, rounds - 1]):
                        if t >= 0:
                            depth[lanes8, pl.ds(t * columns, columns)] = running.pop(t)
                return inner

            lax.fori_loop(0, groups, one_group, 0, unroll=4)
            mixed = jnp.dot(
                mix_ref[layer], depth[...].astype(jnp.bfloat16), preferred_element_type=jnp.float32
            )
            keep = inside(row)
            sums = []
            for t in range(rounds):
                cut = pl.ds(t * columns, columns)
                activated = gelu(mixed[:, t * columns : (t + 1) * columns] + slabs_ref[27 * layers + layer])
                value = (feats[src, row, :, cut] + activated).astype(jnp.bfloat16).astype(jnp.float32)
                value = jnp.where(keep, value, 0.0)
                if last:
                    sums.append(jnp.sum(value * read_ref[...], axis=0, keepdims=True))
                else:
                    feats[dst, row, :, cut] = value
            if last:
                out_ref[row - halo] = jnp.concatenate(sums, axis=0)
            return carry

        lax.fori_loop(layer + 1, extended - layer - 1, one_row, 0)


def run_network(planes, embed_gain, embed_bias, depth_kernel, point_weight, point_bias, read_weight, rows, halo):
    extended, rounds, columns = planes.shape
    layers, channels, _ = depth_kernel.shape
    stacked = jnp.concatenate(
        [
            jnp.transpose(depth_kernel, (0, 2, 1)).reshape(-1, channels),
            point_bias,
            embed_gain[None],
            embed_bias[None],
            read_weight.astype(jnp.float32)[None],
        ],
        axis=0,
    )
    slabs = jnp.broadcast_to(stacked[..., None], stacked.shape + (columns,))
    lane = jnp.arange(columns)
    side = jnp.arange(stacked.shape[0]) % 3
    tap_rows = jnp.arange(stacked.shape[0]) < 27 * layers
    cancel = tap_rows[:, None] & (((side[:, None] == 0) & (lane == 0)) | ((side[:, None] == 2) & (lane == columns - 1)))
    slabs = jnp.where(cancel[:, None, :], 0.0, slabs)
    mix = jnp.transpose(point_weight, (0, 2, 1)).astype(jnp.bfloat16)
    vmem = pl.BlockSpec(memory_space=pltpu.VMEM)
    return pl.pallas_call(
        functools.partial(network_kernel, rows, halo, layers),
        out_shape=jax.ShapeDtypeStruct((rows, rounds, columns), jnp.float32),
        in_specs=[vmem] * 3,
        out_specs=vmem,
        scratch_shapes=[
            pltpu.VMEM((2, extended, channels, rounds * columns), jnp.float32),
            pltpu.VMEM((channels, rounds * columns), jnp.float32),
        ],
        compiler_params=pltpu.CompilerParams(vmem_limit_bytes=56 * 1024 * 1024),
    )(planes, slabs, mix)


def shards(
    axis_names,
    syndromes,
    confidence,
    embed_gain,
    embed_bias,
    depth_kernel,
    point_weight,
    point_bias,
    read_weight,
):
    layers = depth_kernel.shape[0]
    rows = syndromes.shape[1]
    signed_slab = ((2 * syndromes - 1).astype(jnp.float32) * confidence).astype(jnp.bfloat16)
    planes = gather_window(signed_slab, layers, axis_names).astype(jnp.float32)
    logits = run_network(
        planes, embed_gain, embed_bias, depth_kernel, point_weight, point_bias, read_weight, rows, layers
    )
    return jnp.transpose(logits, (1, 0, 2))[None]


def solution(mesh):
    placed = (P("win", "tile", None), P("win", "tile", None), P(), P(), P(), P(), P(), P())
    return jax.shard_map(
        functools.partial(shards, tuple(mesh.axis_names)), mesh=mesh, in_specs=placed, out_specs=P("win", None, "tile", None), check_vma=False
    )
```

```python
import functools

import jax
import jax.numpy as jnp
from jax import lax
from jax.experimental import pallas as pl
from jax.experimental.pallas import tpu as pltpu
from jax.sharding import PartitionSpec as P

WINDOW = 16
COMMIT = 2


def exchange_kernel(axis_names, halo, slab_ref, out_ref, held, recv_sem, send_sem, local_sem):
    tiles, wins = lax.axis_size("tile"), lax.axis_size("win")
    tile, win = lax.axis_index("tile"), lax.axis_index("win")
    pieces, rows = slab_ref.shape[0], slab_ref.shape[1]
    span = held.shape[0]

    def device(tile_index, win_index):
        place = {"tile": tile_index, "win": win_index}
        return tuple(place[name] for name in axis_names)

    mesh_ids = pl.DeviceIdType.MESH
    blank = jnp.zeros((span, halo) + held.shape[2:], held.dtype)

    @pl.when(tile == 0)
    def _():
        held[:, pl.ds(0, halo)] = blank

    @pl.when(tile == tiles - 1)
    def _():
        held[:, pl.ds(rows + halo, halo)] = blank

    neighbour_tiles = 1 + (tile > 0).astype(jnp.int32) + (tile < tiles - 1).astype(jnp.int32)
    barrier = pltpu.get_barrier_semaphore()
    for shift in (-1, 0, 1):
        for other in range(wins):
            there = tile + shift
            partner = (there >= 0) & (there < tiles)
            if shift == 0:
                partner = partner & (win != other)

            @pl.when(partner)
            def _():
                pl.semaphore_signal(barrier, 1, device_id=device(there, other), device_id_type=mesh_ids)

    pl.semaphore_wait(barrier, neighbour_tiles * wins - 1)

    parts = ((-1, 0, rows + halo, halo, 0), (0, 0, halo, rows, 1), (1, rows - halo, 0, halo, 0))
    started = []
    for piece in range(pieces):
        global_piece = win * pieces + piece
        for other in range(wins):
            offset = global_piece - other
            needed = (offset >= 0) & (offset < span)
            offset = jnp.clip(offset, 0, span - 1)
            for shift, src_row, dst_row, count, kind in parts:
                there = tile + shift
                ok = needed & (there >= 0) & (there < tiles)
                there = jnp.clip(there, 0, tiles - 1)
                src = slab_ref.at[pl.ds(piece, 1), pl.ds(src_row, count)]
                dst = held.at[pl.ds(offset, 1), pl.ds(dst_row, count)]
                if shift == 0:
                    local = ok & (win == other)
                    remote = ok & (win != other)
                    copy_local = pltpu.make_async_copy(src, dst, local_sem)

                    @pl.when(local)
                    def _():
                        copy_local.start()
                        copy_local.wait()
                else:
                    remote = ok
                copy = pltpu.make_async_remote_copy(
                    src_ref=src,
                    dst_ref=dst,
                    send_sem=send_sem.at[piece, other, shift + 1],
                    recv_sem=recv_sem.at[offset, shift + 1],
                    device_id=device(there, other),
                    device_id_type=mesh_ids,
                )

                @pl.when(remote)
                def _():
                    copy.start()

                started.append((remote, copy))

    for remote, copy in started:

        @pl.when(remote)
        def _():
            copy.wait_send()

    for step in range(span):
        source_win = (win + step) // pieces
        for shift, src_row, dst_row, count, kind in parts:
            there = tile - shift
            ok = (there >= 0) & (there < tiles)
            if shift == 0:
                ok = ok & (source_win != win)
            probe = pltpu.make_async_remote_copy(
                src_ref=slab_ref.at[pl.ds(0, 1), pl.ds(src_row, count)],
                dst_ref=held.at[pl.ds(0, 1), pl.ds(dst_row, count)],
                send_sem=send_sem.at[0, 0, shift + 1],
                recv_sem=recv_sem.at[step, shift + 1],
                device_id=device(there, win),
                device_id_type=mesh_ids,
            )

            @pl.when(ok)
            def _():
                probe.wait_recv()

    out_ref[...] = held[...]


def gather_window(signed_slab, halo, axis_names):
    rounds, rows, columns = signed_slab.shape
    pieces = rounds // COMMIT
    span = WINDOW // COMMIT
    cut = jnp.transpose(signed_slab.reshape(pieces, COMMIT, rows, columns), (0, 2, 1, 3))
    shape = (span, rows + 2 * halo, COMMIT, columns)
    held = pl.pallas_call(
        functools.partial(exchange_kernel, axis_names, halo),
        out_shape=jax.ShapeDtypeStruct(shape, signed_slab.dtype),
        in_specs=[pl.BlockSpec(memory_space=pltpu.VMEM)],
        out_specs=pl.BlockSpec(memory_space=pltpu.VMEM),
        scratch_shapes=[
            pltpu.VMEM(shape, signed_slab.dtype),
            pltpu.SemaphoreType.DMA((span, 3)),
            pltpu.SemaphoreType.DMA((pieces, lax.axis_size("win"), 3)),
            pltpu.SemaphoreType.DMA,
        ],
        compiler_params=pltpu.CompilerParams(collective_id=0, has_side_effects=True),
    )(cut)
    return held


def gelu(value):
    return 0.5 * value * (1.0 + jnp.tanh(0.7978845608028654 * (value + 0.044715 * (value * value * value))))


def network_kernel(rows, halo, layers, planes_ref, slabs_ref, mix_ref, out_ref, feats, depth):
    span, extended, commit, columns = planes_ref.shape
    rounds = span * commit
    channels = slabs_ref.shape[1]
    tail = 28 * layers
    gain_ref, bias_ref, read_ref = slabs_ref.at[tail], slabs_ref.at[tail + 1], slabs_ref.at[tail + 2]
    groups = channels // 8
    tiles = lax.axis_size("tile")
    first_row = lax.axis_index("tile") * rows - halo

    def inside(row):
        plane_row = first_row + row
        return (plane_row >= 0) & (plane_row < rows * tiles)

    def embed(row, carry):
        keep = inside(row)
        for t in range(rounds):
            plane = planes_ref[t // commit, row, pl.ds(t % commit, 1), :].astype(jnp.float32)
            value = plane * gain_ref[...] + bias_ref[...]
            value = value.astype(jnp.bfloat16).astype(jnp.float32)
            feats[0, row, :, pl.ds(t * columns, columns)] = jnp.where(keep, value, 0.0)
        return carry

    lax.fori_loop(0, extended, embed, 0)

    def spread(value):
        return (pltpu.roll(value, 1, 1), value, pltpu.roll(value, columns - 1, 1))

    for layer in range(layers):
        src, dst = layer % 2, (layer + 1) % 2
        last = layer == layers - 1

        def one_row(row, carry, layer=layer, src=src, dst=dst, last=last):
            def one_group(group, inner):
                lanes8 = pl.ds(pl.multiple_of(group * 8, 8), 8)
                weights = [slabs_ref[27 * layer + tap, lanes8, :] for tap in range(27)]
                running = {}
                for source in range(rounds):
                    cut = pl.ds(source * columns, columns)
                    held = [spread(feats[src, row - 1 + b, lanes8, cut]) for b in range(3)]
                    for a in range(3):
                        t = source - a + 1
                        if t < 0 or t >= rounds:
                            continue
                        for b in range(3):
                            for e in range(3):
                                term = weights[9 * a + 3 * b + e] * held[b][e]
                                running[t] = term if t not in running else running[t] + term
                    done = source - 1 if source < rounds - 1 else None
                    for t in ([done] if done is not None else [rounds - 2, rounds - 1]):
                        if t >= 0:
                            depth[lanes8, pl.ds(t * columns, columns)] = running.pop(t)
                return inner

            lax.fori_loop(0, groups, one_group, 0, unroll=8)
            mixed = jnp.dot(
                mix_ref[layer], depth[...].astype(jnp.bfloat16), preferred_element_type=jnp.float32
            )
            keep = inside(row)
            sums = []
            for t in range(rounds):
                cut = pl.ds(t * columns, columns)
                activated = gelu(mixed[:, t * columns : (t + 1) * columns] + slabs_ref[27 * layers + layer])
                value = (feats[src, row, :, cut] + activated).astype(jnp.bfloat16).astype(jnp.float32)
                value = jnp.where(keep, value, 0.0)
                if last:
                    sums.append(jnp.sum(value * read_ref[...], axis=0, keepdims=True))
                else:
                    feats[dst, row, :, cut] = value
            if last:
                out_ref[row - halo] = jnp.concatenate(sums, axis=0)
            return carry

        lax.fori_loop(layer + 1, extended - layer - 1, one_row, 0)


def run_network(planes, embed_gain, embed_bias, depth_kernel, point_weight, point_bias, read_weight, rows, halo):
    span, extended, commit, columns = planes.shape
    rounds = span * commit
    layers, channels, _ = depth_kernel.shape
    stacked = jnp.concatenate(
        [
            jnp.transpose(depth_kernel, (0, 2, 1)).reshape(-1, channels),
            point_bias,
            embed_gain[None],
            embed_bias[None],
            read_weight.astype(jnp.float32)[None],
        ],
        axis=0,
    )
    slabs = jnp.broadcast_to(stacked[..., None], stacked.shape + (columns,))
    lane = jnp.arange(columns)
    side = jnp.arange(stacked.shape[0]) % 3
    tap_rows = jnp.arange(stacked.shape[0]) < 27 * layers
    cancel = tap_rows[:, None] & (((side[:, None] == 0) & (lane == 0)) | ((side[:, None] == 2) & (lane == columns - 1)))
    slabs = jnp.where(cancel[:, None, :], 0.0, slabs)
    mix = jnp.transpose(point_weight, (0, 2, 1)).astype(jnp.bfloat16)
    vmem = pl.BlockSpec(memory_space=pltpu.VMEM)
    return pl.pallas_call(
        functools.partial(network_kernel, rows, halo, layers),
        out_shape=jax.ShapeDtypeStruct((rows, rounds, columns), jnp.float32),
        in_specs=[vmem] * 3,
        out_specs=vmem,
        scratch_shapes=[
            pltpu.VMEM((2, extended, channels, rounds * columns), jnp.float32),
            pltpu.VMEM((channels, rounds * columns), jnp.float32),
        ],
        compiler_params=pltpu.CompilerParams(vmem_limit_bytes=56 * 1024 * 1024),
    )(planes, slabs, mix)


def shards(
    axis_names,
    syndromes,
    confidence,
    embed_gain,
    embed_bias,
    depth_kernel,
    point_weight,
    point_bias,
    read_weight,
):
    layers = depth_kernel.shape[0]
    rows = syndromes.shape[1]
    signed_slab = ((2 * syndromes - 1).astype(jnp.float32) * confidence).astype(jnp.bfloat16)
    planes = gather_window(signed_slab, layers, axis_names)
    logits = run_network(
        planes, embed_gain, embed_bias, depth_kernel, point_weight, point_bias, read_weight, rows, layers
    )
    return jnp.transpose(logits, (1, 0, 2))[None]


def solution(mesh):
    placed = (P("win", "tile", None), P("win", "tile", None), P(), P(), P(), P(), P(), P())
    return jax.shard_map(
        functools.partial(shards, tuple(mesh.axis_names)), mesh=mesh, in_specs=placed, out_specs=P("win", None, "tile", None), check_vma=False
    )
```

```python
import functools

import jax
import jax.numpy as jnp
from jax import lax
from jax.experimental import pallas as pl
from jax.experimental.pallas import tpu as pltpu
from jax.sharding import PartitionSpec as P

WINDOW = 16
COMMIT = 2


def exchange_kernel(axis_names, halo, slab_ref, out_ref, held, recv_sem, send_sem, local_sem):
    tiles, wins = lax.axis_size("tile"), lax.axis_size("win")
    tile, win = lax.axis_index("tile"), lax.axis_index("win")
    pieces, rows = slab_ref.shape[0], slab_ref.shape[1]
    span = held.shape[0]

    def device(tile_index, win_index):
        place = {"tile": tile_index, "win": win_index}
        return tuple(place[name] for name in axis_names)

    mesh_ids = pl.DeviceIdType.MESH
    blank = jnp.zeros((span, halo) + held.shape[2:], held.dtype)

    @pl.when(tile == 0)
    def _():
        held[:, pl.ds(0, halo)] = blank

    @pl.when(tile == tiles - 1)
    def _():
        held[:, pl.ds(rows + halo, halo)] = blank

    neighbour_tiles = 1 + (tile > 0).astype(jnp.int32) + (tile < tiles - 1).astype(jnp.int32)
    barrier = pltpu.get_barrier_semaphore()
    for shift in (-1, 0, 1):
        for other in range(wins):
            there = tile + shift
            partner = (there >= 0) & (there < tiles)
            if shift == 0:
                partner = partner & (win != other)

            @pl.when(partner)
            def _():
                pl.semaphore_signal(barrier, 1, device_id=device(there, other), device_id_type=mesh_ids)

    pl.semaphore_wait(barrier, neighbour_tiles * wins - 1)

    parts = ((-1, 0, rows + halo, halo, 0), (0, 0, halo, rows, 1), (1, rows - halo, 0, halo, 0))
    started = []
    for piece in range(pieces):
        global_piece = win * pieces + piece
        for other in range(wins):
            offset = global_piece - other
            needed = (offset >= 0) & (offset < span)
            offset = jnp.clip(offset, 0, span - 1)
            for shift, src_row, dst_row, count, kind in parts:
                there = tile + shift
                ok = needed & (there >= 0) & (there < tiles)
                there = jnp.clip(there, 0, tiles - 1)
                src = slab_ref.at[pl.ds(piece, 1), pl.ds(src_row, count)]
                dst = held.at[pl.ds(offset, 1), pl.ds(dst_row, count)]
                if shift == 0:
                    local = ok & (win == other)
                    remote = ok & (win != other)
                    copy_local = pltpu.make_async_copy(src, dst, local_sem)

                    @pl.when(local)
                    def _():
                        copy_local.start()
                        copy_local.wait()
                else:
                    remote = ok
                copy = pltpu.make_async_remote_copy(
                    src_ref=src,
                    dst_ref=dst,
                    send_sem=send_sem.at[piece, other, shift + 1],
                    recv_sem=recv_sem.at[offset, shift + 1],
                    device_id=device(there, other),
                    device_id_type=mesh_ids,
                )

                @pl.when(remote)
                def _():
                    copy.start()

                started.append((remote, copy))

    for remote, copy in started:

        @pl.when(remote)
        def _():
            copy.wait_send()

    for step in range(span):
        source_win = (win + step) // pieces
        for shift, src_row, dst_row, count, kind in parts:
            there = tile - shift
            ok = (there >= 0) & (there < tiles)
            if shift == 0:
                ok = ok & (source_win != win)
            probe = pltpu.make_async_remote_copy(
                src_ref=slab_ref.at[pl.ds(0, 1), pl.ds(src_row, count)],
                dst_ref=held.at[pl.ds(0, 1), pl.ds(dst_row, count)],
                send_sem=send_sem.at[0, 0, shift + 1],
                recv_sem=recv_sem.at[step, shift + 1],
                device_id=device(there, win),
                device_id_type=mesh_ids,
            )

            @pl.when(ok)
            def _():
                probe.wait_recv()

    out_ref[...] = held[...]


def gather_window(signed_slab, halo, axis_names):
    rounds, rows, columns = signed_slab.shape
    pieces = rounds // COMMIT
    span = WINDOW // COMMIT
    cut = jnp.transpose(signed_slab.reshape(pieces, COMMIT, rows, columns), (0, 2, 1, 3))
    shape = (span, rows + 2 * halo, COMMIT, columns)
    held = pl.pallas_call(
        functools.partial(exchange_kernel, axis_names, halo),
        out_shape=jax.ShapeDtypeStruct(shape, signed_slab.dtype),
        in_specs=[pl.BlockSpec(memory_space=pltpu.VMEM)],
        out_specs=pl.BlockSpec(memory_space=pltpu.VMEM),
        scratch_shapes=[
            pltpu.VMEM(shape, signed_slab.dtype),
            pltpu.SemaphoreType.DMA((span, 3)),
            pltpu.SemaphoreType.DMA((pieces, lax.axis_size("win"), 3)),
            pltpu.SemaphoreType.DMA,
        ],
        compiler_params=pltpu.CompilerParams(collective_id=0, has_side_effects=True),
    )(cut)
    return held


def gelu(value):
    return 0.5 * value * (1.0 + jnp.tanh(0.7978845608028654 * (value + 0.044715 * (value * value * value))))


def network_kernel(rows, halo, layers, planes_ref, compact_ref, mix_ref, out_ref, feats, depth, slabs_ref):
    span, extended, commit, columns = planes_ref.shape
    rounds = span * commit
    channels = slabs_ref.shape[1]
    lane = lax.broadcasted_iota(jnp.int32, (channels, columns), 1)
    for k in range(slabs_ref.shape[0]):
        slab = jnp.broadcast_to(compact_ref[:, pl.ds(k, 1)], (channels, columns))
        if k < 27 * layers and k % 3 == 0:
            slab = jnp.where(lane == 0, 0.0, slab)
        if k < 27 * layers and k % 3 == 2:
            slab = jnp.where(lane == columns - 1, 0.0, slab)
        slabs_ref[k] = slab
    tail = 28 * layers
    gain_ref, bias_ref, read_ref = slabs_ref.at[tail], slabs_ref.at[tail + 1], slabs_ref.at[tail + 2]
    groups = channels // 8
    tiles = lax.axis_size("tile")
    first_row = lax.axis_index("tile") * rows - halo

    def inside(row):
        plane_row = first_row + row
        return (plane_row >= 0) & (plane_row < rows * tiles)

    def embed(row, carry):
        keep = inside(row)
        for t in range(rounds):
            plane = planes_ref[t // commit, row, pl.ds(t % commit, 1), :].astype(jnp.float32)
            value = plane * gain_ref[...] + bias_ref[...]
            value = value.astype(jnp.bfloat16).astype(jnp.float32)
            feats[0, row, :, pl.ds(t * columns, columns)] = jnp.where(keep, value, 0.0)
        return carry

    lax.fori_loop(0, extended, embed, 0)

    def spread(value):
        return (pltpu.roll(value, 1, 1), value, pltpu.roll(value, columns - 1, 1))

    for layer in range(layers):
        src, dst = layer % 2, (layer + 1) % 2
        last = layer == layers - 1

        def one_row(row, carry, layer=layer, src=src, dst=dst, last=last):
            def one_group(group, inner):
                lanes8 = pl.ds(pl.multiple_of(group * 8, 8), 8)
                weights = [slabs_ref[27 * layer + tap, lanes8, :] for tap in range(27)]
                running = {}
                for source in range(rounds):
                    cut = pl.ds(source * columns, columns)
                    held = [spread(feats[src, row - 1 + b, lanes8, cut]) for b in range(3)]
                    for a in range(3):
                        t = source - a + 1
                        if t < 0 or t >= rounds:
                            continue
                        for b in range(3):
                            for e in range(3):
                                term = weights[9 * a + 3 * b + e] * held[b][e]
                                running[t] = term if t not in running else running[t] + term
                    done = source - 1 if source < rounds - 1 else None
                    for t in ([done] if done is not None else [rounds - 2, rounds - 1]):
                        if t >= 0:
                            depth[lanes8, pl.ds(t * columns, columns)] = running.pop(t)
                return inner

            lax.fori_loop(0, groups, one_group, 0, unroll=8)
            mixed = jnp.dot(
                mix_ref[layer], depth[...].astype(jnp.bfloat16), preferred_element_type=jnp.float32
            )
            keep = inside(row)
            sums = []
            for t in range(rounds):
                cut = pl.ds(t * columns, columns)
                activated = gelu(mixed[:, t * columns : (t + 1) * columns] + slabs_ref[27 * layers + layer])
                value = (feats[src, row, :, cut] + activated).astype(jnp.bfloat16).astype(jnp.float32)
                value = jnp.where(keep, value, 0.0)
                if last:
                    sums.append(jnp.sum(value * read_ref[...], axis=0, keepdims=True))
                else:
                    feats[dst, row, :, cut] = value
            if last:
                out_ref[row - halo] = jnp.concatenate(sums, axis=0)
            return carry

        lax.fori_loop(layer + 1, extended - layer - 1, one_row, 0)


def run_network(planes, embed_gain, embed_bias, depth_kernel, point_weight, point_bias, read_weight, rows, halo):
    span, extended, commit, columns = planes.shape
    rounds = span * commit
    layers, channels, _ = depth_kernel.shape
    stacked = jnp.concatenate(
        [
            jnp.transpose(depth_kernel, (0, 2, 1)).reshape(-1, channels),
            point_bias,
            embed_gain[None],
            embed_bias[None],
            read_weight.astype(jnp.float32)[None],
        ],
        axis=0,
    )
    compact = jnp.transpose(stacked)
    mix = jnp.transpose(point_weight, (0, 2, 1)).astype(jnp.bfloat16)
    vmem = pl.BlockSpec(memory_space=pltpu.VMEM)
    return pl.pallas_call(
        functools.partial(network_kernel, rows, halo, layers),
        out_shape=jax.ShapeDtypeStruct((rows, rounds, columns), jnp.float32),
        in_specs=[vmem] * 3,
        out_specs=vmem,
        scratch_shapes=[
            pltpu.VMEM((2, extended, channels, rounds * columns), jnp.float32),
            pltpu.VMEM((channels, rounds * columns), jnp.float32),
            pltpu.VMEM((stacked.shape[0], channels, columns), jnp.float32),
        ],
        compiler_params=pltpu.CompilerParams(vmem_limit_bytes=56 * 1024 * 1024),
    )(planes, compact, mix)


def shards(
    axis_names,
    syndromes,
    confidence,
    embed_gain,
    embed_bias,
    depth_kernel,
    point_weight,
    point_bias,
    read_weight,
):
    layers = depth_kernel.shape[0]
    rows = syndromes.shape[1]
    signed_slab = ((2 * syndromes - 1).astype(jnp.float32) * confidence).astype(jnp.bfloat16)
    planes = gather_window(signed_slab, layers, axis_names)
    logits = run_network(
        planes, embed_gain, embed_bias, depth_kernel, point_weight, point_bias, read_weight, rows, layers
    )
    return jnp.transpose(logits, (1, 0, 2))[None]


def solution(mesh):
    placed = (P("win", "tile", None), P("win", "tile", None), P(), P(), P(), P(), P(), P())
    return jax.shard_map(
        functools.partial(shards, tuple(mesh.axis_names)), mesh=mesh, in_specs=placed, out_specs=P("win", None, "tile", None), check_vma=False
    )
```

```python
import functools

import jax
import jax.numpy as jnp
from jax import lax
from jax.experimental import pallas as pl
from jax.experimental.pallas import tpu as pltpu
from jax.sharding import PartitionSpec as P

WINDOW = 16
COMMIT = 2


def exchange_kernel(axis_names, halo, slab_ref, out_ref, held, recv_sem, send_sem, local_sem):
    tiles, wins = lax.axis_size("tile"), lax.axis_size("win")
    tile, win = lax.axis_index("tile"), lax.axis_index("win")
    pieces, rows = slab_ref.shape[0], slab_ref.shape[1]
    span = held.shape[0]

    def device(tile_index, win_index):
        place = {"tile": tile_index, "win": win_index}
        return tuple(place[name] for name in axis_names)

    mesh_ids = pl.DeviceIdType.MESH
    blank = jnp.zeros((span, halo) + held.shape[2:], held.dtype)

    @pl.when(tile == 0)
    def _():
        held[:, pl.ds(0, halo)] = blank

    @pl.when(tile == tiles - 1)
    def _():
        held[:, pl.ds(rows + halo, halo)] = blank

    neighbour_tiles = 1 + (tile > 0).astype(jnp.int32) + (tile < tiles - 1).astype(jnp.int32)
    barrier = pltpu.get_barrier_semaphore()
    for shift in (-1, 0, 1):
        for other in range(wins):
            there = tile + shift
            partner = (there >= 0) & (there < tiles)
            if shift == 0:
                partner = partner & (win != other)

            @pl.when(partner)
            def _():
                pl.semaphore_signal(barrier, 1, device_id=device(there, other), device_id_type=mesh_ids)

    pl.semaphore_wait(barrier, neighbour_tiles * wins - 1)

    parts = ((-1, 0, rows + halo, halo, 0), (0, 0, halo, rows, 1), (1, rows - halo, 0, halo, 0))
    started = []
    for piece in range(pieces):
        global_piece = win * pieces + piece
        for other in range(wins):
            offset = global_piece - other
            needed = (offset >= 0) & (offset < span)
            offset = jnp.clip(offset, 0, span - 1)
            for shift, src_row, dst_row, count, kind in parts:
                there = tile + shift
                ok = needed & (there >= 0) & (there < tiles)
                there = jnp.clip(there, 0, tiles - 1)
                src = slab_ref.at[pl.ds(piece, 1), pl.ds(src_row, count)]
                dst = held.at[pl.ds(offset, 1), pl.ds(dst_row, count)]
                if shift == 0:
                    local = ok & (win == other)
                    remote = ok & (win != other)
                    copy_local = pltpu.make_async_copy(src, dst, local_sem)

                    @pl.when(local)
                    def _():
                        copy_local.start()
                        copy_local.wait()
                else:
                    remote = ok
                copy = pltpu.make_async_remote_copy(
                    src_ref=src,
                    dst_ref=dst,
                    send_sem=send_sem.at[piece, other, shift + 1],
                    recv_sem=recv_sem.at[offset, shift + 1],
                    device_id=device(there, other),
                    device_id_type=mesh_ids,
                )

                @pl.when(remote)
                def _():
                    copy.start()

                started.append((remote, copy))

    for remote, copy in started:

        @pl.when(remote)
        def _():
            copy.wait_send()

    for step in range(span):
        source_win = (win + step) // pieces
        for shift, src_row, dst_row, count, kind in parts:
            there = tile - shift
            ok = (there >= 0) & (there < tiles)
            if shift == 0:
                ok = ok & (source_win != win)
            probe = pltpu.make_async_remote_copy(
                src_ref=slab_ref.at[pl.ds(0, 1), pl.ds(src_row, count)],
                dst_ref=held.at[pl.ds(0, 1), pl.ds(dst_row, count)],
                send_sem=send_sem.at[0, 0, shift + 1],
                recv_sem=recv_sem.at[step, shift + 1],
                device_id=device(there, win),
                device_id_type=mesh_ids,
            )

            @pl.when(ok)
            def _():
                probe.wait_recv()

    out_ref[...] = held[...]


def gather_window(signed_slab, halo, axis_names):
    rounds, rows, columns = signed_slab.shape
    pieces = rounds // COMMIT
    span = WINDOW // COMMIT
    cut = jnp.transpose(signed_slab.reshape(pieces, COMMIT, rows, columns), (0, 2, 1, 3))
    shape = (span, rows + 2 * halo, COMMIT, columns)
    held = pl.pallas_call(
        functools.partial(exchange_kernel, axis_names, halo),
        out_shape=jax.ShapeDtypeStruct(shape, signed_slab.dtype),
        in_specs=[pl.BlockSpec(memory_space=pltpu.VMEM)],
        out_specs=pl.BlockSpec(memory_space=pltpu.VMEM),
        scratch_shapes=[
            pltpu.VMEM(shape, signed_slab.dtype),
            pltpu.SemaphoreType.DMA((span, 3)),
            pltpu.SemaphoreType.DMA((pieces, lax.axis_size("win"), 3)),
            pltpu.SemaphoreType.DMA,
        ],
        compiler_params=pltpu.CompilerParams(collective_id=0, has_side_effects=True),
    )(cut)
    return held


def gelu(value):
    half = 0.5 * value
    inner = value * (0.7978845608028654 + 0.035677408136300125 * (value * value))
    return half + half * jnp.tanh(inner)


def network_kernel(rows, halo, layers, planes_ref, slabs_hbm, mix_ref, out_ref, feats, depth, slabs_ref, slab_sems):
    span, extended, commit, columns = planes_ref.shape
    rounds = span * commit
    channels = slabs_ref.shape[1]
    early = 3 + layers + 27
    total_slabs = slabs_ref.shape[0]
    fetch_early = pltpu.make_async_copy(
        slabs_hbm.at[pl.ds(0, early)], slabs_ref.at[pl.ds(0, early)], slab_sems.at[0]
    )
    fetch_late = pltpu.make_async_copy(
        slabs_hbm.at[pl.ds(early, total_slabs - early)],
        slabs_ref.at[pl.ds(early, total_slabs - early)],
        slab_sems.at[1],
    )
    fetch_early.start()
    fetch_late.start()
    gain_ref, bias_ref, read_ref = slabs_ref.at[0], slabs_ref.at[1], slabs_ref.at[2]
    groups = channels // 8
    tiles = lax.axis_size("tile")
    first_row = lax.axis_index("tile") * rows - halo
    fetch_early.wait()

    def inside(row):
        plane_row = first_row + row
        return (plane_row >= 0) & (plane_row < rows * tiles)

    def embed(row, carry):
        keep = inside(row)
        for t in range(rounds):
            plane = planes_ref[t // commit, row, pl.ds(t % commit, 1), :].astype(jnp.float32)
            value = plane * gain_ref[...] + bias_ref[...]
            value = value.astype(jnp.bfloat16).astype(jnp.float32)
            feats[0, row, :, pl.ds(t * columns, columns)] = jnp.where(keep, value, 0.0)
        return carry

    lax.fori_loop(0, extended, embed, 0)

    def spread(value):
        return (pltpu.roll(value, 1, 1), value, pltpu.roll(value, columns - 1, 1))

    for layer in range(layers):
        if layer == 1:
            fetch_late.wait()
        src, dst = layer % 2, (layer + 1) % 2
        last = layer == layers - 1

        def one_row(row, carry, layer=layer, src=src, dst=dst, last=last):
            def one_group(group, inner):
                lanes8 = pl.ds(pl.multiple_of(group * 8, 8), 8)
                weights = [slabs_ref[3 + layers + 27 * layer + tap, lanes8, :] for tap in range(27)]
                running = {}
                for source in range(rounds):
                    cut = pl.ds(source * columns, columns)
                    held = [spread(feats[src, row - 1 + b, lanes8, cut]) for b in range(3)]
                    for a in range(3):
                        t = source - a + 1
                        if t < 0 or t >= rounds:
                            continue
                        for b in range(3):
                            for e in range(3):
                                term = weights[9 * a + 3 * b + e] * held[b][e]
                                running[t] = term if t not in running else running[t] + term
                    done = source - 1 if source < rounds - 1 else None
                    for t in ([done] if done is not None else [rounds - 2, rounds - 1]):
                        if t >= 0:
                            depth[lanes8, pl.ds(t * columns, columns)] = running.pop(t)
                return inner

            lax.fori_loop(0, groups, one_group, 0, unroll=8)
            mixed = jnp.dot(
                mix_ref[layer], depth[...].astype(jnp.bfloat16), preferred_element_type=jnp.float32
            )
            keep = inside(row)
            sums = []
            for t in range(rounds):
                cut = pl.ds(t * columns, columns)
                activated = gelu(mixed[:, t * columns : (t + 1) * columns] + slabs_ref[3 + layer])
                value = (feats[src, row, :, cut] + activated).astype(jnp.bfloat16).astype(jnp.float32)
                value = jnp.where(keep, value, 0.0)
                if last:
                    sums.append(jnp.sum(value * read_ref[...], axis=0, keepdims=True))
                else:
                    feats[dst, row, :, cut] = value
            if last:
                out_ref[row - halo] = jnp.concatenate(sums, axis=0)
            return carry

        lax.fori_loop(layer + 1, extended - layer - 1, one_row, 0)


def run_network(planes, embed_gain, embed_bias, depth_kernel, point_weight, point_bias, read_weight, rows, halo):
    span, extended, commit, columns = planes.shape
    rounds = span * commit
    layers, channels, _ = depth_kernel.shape
    stacked = jnp.concatenate(
        [
            embed_gain[None],
            embed_bias[None],
            read_weight.astype(jnp.float32)[None],
            point_bias,
            jnp.transpose(depth_kernel, (0, 2, 1)).reshape(-1, channels),
        ],
        axis=0,
    )
    slabs = jnp.broadcast_to(stacked[..., None], stacked.shape + (columns,))
    lane = jnp.arange(columns)
    tap_index = jnp.arange(stacked.shape[0]) - (3 + layers)
    side = tap_index % 3
    tap_rows = tap_index >= 0
    cancel = tap_rows[:, None] & (((side[:, None] == 0) & (lane == 0)) | ((side[:, None] == 2) & (lane == columns - 1)))
    slabs = jnp.where(cancel[:, None, :], 0.0, slabs)
    mix = jnp.transpose(point_weight, (0, 2, 1)).astype(jnp.bfloat16)
    vmem = pl.BlockSpec(memory_space=pltpu.VMEM)
    return pl.pallas_call(
        functools.partial(network_kernel, rows, halo, layers),
        out_shape=jax.ShapeDtypeStruct((rows, rounds, columns), jnp.float32),
        in_specs=[vmem, pl.BlockSpec(memory_space=pl.ANY), vmem],
        out_specs=vmem,
        scratch_shapes=[
            pltpu.VMEM((2, extended, channels, rounds * columns), jnp.float32),
            pltpu.VMEM((channels, rounds * columns), jnp.float32),
            pltpu.VMEM(slabs.shape, jnp.float32),
            pltpu.SemaphoreType.DMA((2,)),
        ],
        compiler_params=pltpu.CompilerParams(vmem_limit_bytes=56 * 1024 * 1024),
    )(planes, slabs, mix)


def shards(
    axis_names,
    syndromes,
    confidence,
    embed_gain,
    embed_bias,
    depth_kernel,
    point_weight,
    point_bias,
    read_weight,
):
    layers = depth_kernel.shape[0]
    rows = syndromes.shape[1]
    signed_slab = ((2 * syndromes - 1).astype(jnp.float32) * confidence).astype(jnp.bfloat16)
    planes = gather_window(signed_slab, layers, axis_names)
    logits = run_network(
        planes, embed_gain, embed_bias, depth_kernel, point_weight, point_bias, read_weight, rows, layers
    )
    return jnp.transpose(logits, (1, 0, 2))[None]


def solution(mesh):
    placed = (P("win", "tile", None), P("win", "tile", None), P(), P(), P(), P(), P(), P())
    return jax.shard_map(
        functools.partial(shards, tuple(mesh.axis_names)), mesh=mesh, in_specs=placed, out_specs=P("win", None, "tile", None), check_vma=False
    )
```

```python
import functools

import jax
import jax.numpy as jnp
from jax import lax
from jax.experimental import pallas as pl
from jax.experimental.pallas import tpu as pltpu
from jax.sharding import PartitionSpec as P

WINDOW = 16
COMMIT = 2


def exchange_kernel(axis_names, halo, slab_ref, out_ref, held, recv_sem, send_sem, local_sem):
    tiles, wins = lax.axis_size("tile"), lax.axis_size("win")
    tile, win = lax.axis_index("tile"), lax.axis_index("win")
    pieces, rows = slab_ref.shape[0], slab_ref.shape[1]
    span = held.shape[0]

    def device(tile_index, win_index):
        place = {"tile": tile_index, "win": win_index}
        return tuple(place[name] for name in axis_names)

    mesh_ids = pl.DeviceIdType.MESH
    blank = jnp.zeros((span, halo) + held.shape[2:], held.dtype)

    @pl.when(tile == 0)
    def _():
        held[:, pl.ds(0, halo)] = blank

    @pl.when(tile == tiles - 1)
    def _():
        held[:, pl.ds(rows + halo, halo)] = blank

    neighbour_tiles = 1 + (tile > 0).astype(jnp.int32) + (tile < tiles - 1).astype(jnp.int32)
    barrier = pltpu.get_barrier_semaphore()
    for shift in (-1, 0, 1):
        for other in range(wins):
            there = tile + shift
            partner = (there >= 0) & (there < tiles)
            if shift == 0:
                partner = partner & (win != other)

            @pl.when(partner)
            def _():
                pl.semaphore_signal(barrier, 1, device_id=device(there, other), device_id_type=mesh_ids)

    pl.semaphore_wait(barrier, neighbour_tiles * wins - 1)

    parts = ((-1, 0, rows + halo, halo, 0), (0, 0, halo, rows, 1), (1, rows - halo, 0, halo, 0))
    started = []
    for piece in range(pieces):
        global_piece = win * pieces + piece
        for other in range(wins):
            offset = global_piece - other
            needed = (offset >= 0) & (offset < span)
            offset = jnp.clip(offset, 0, span - 1)
            for shift, src_row, dst_row, count, kind in parts:
                there = tile + shift
                ok = needed & (there >= 0) & (there < tiles)
                there = jnp.clip(there, 0, tiles - 1)
                src = slab_ref.at[pl.ds(piece, 1), pl.ds(src_row, count)]
                dst = held.at[pl.ds(offset, 1), pl.ds(dst_row, count)]
                if shift == 0:
                    local = ok & (win == other)
                    remote = ok & (win != other)
                    copy_local = pltpu.make_async_copy(src, dst, local_sem)

                    @pl.when(local)
                    def _():
                        copy_local.start()
                        copy_local.wait()
                else:
                    remote = ok
                copy = pltpu.make_async_remote_copy(
                    src_ref=src,
                    dst_ref=dst,
                    send_sem=send_sem.at[piece, other, shift + 1],
                    recv_sem=recv_sem.at[offset, shift + 1],
                    device_id=device(there, other),
                    device_id_type=mesh_ids,
                )

                @pl.when(remote)
                def _():
                    copy.start()

                started.append((remote, copy))

    for remote, copy in started:

        @pl.when(remote)
        def _():
            copy.wait_send()

    for step in range(span):
        source_win = (win + step) // pieces
        for shift, src_row, dst_row, count, kind in parts:
            there = tile - shift
            ok = (there >= 0) & (there < tiles)
            if shift == 0:
                ok = ok & (source_win != win)
            probe = pltpu.make_async_remote_copy(
                src_ref=slab_ref.at[pl.ds(0, 1), pl.ds(src_row, count)],
                dst_ref=held.at[pl.ds(0, 1), pl.ds(dst_row, count)],
                send_sem=send_sem.at[0, 0, shift + 1],
                recv_sem=recv_sem.at[step, shift + 1],
                device_id=device(there, win),
                device_id_type=mesh_ids,
            )

            @pl.when(ok)
            def _():
                probe.wait_recv()

    out_ref[...] = held[...]


def gather_window(signed_slab, halo, axis_names):
    rounds, rows, columns = signed_slab.shape
    pieces = rounds // COMMIT
    span = WINDOW // COMMIT
    cut = jnp.transpose(signed_slab.reshape(pieces, COMMIT, rows, columns), (0, 2, 1, 3))
    shape = (span, rows + 2 * halo, COMMIT, columns)
    held = pl.pallas_call(
        functools.partial(exchange_kernel, axis_names, halo),
        out_shape=jax.ShapeDtypeStruct(shape, signed_slab.dtype),
        in_specs=[pl.BlockSpec(memory_space=pltpu.VMEM)],
        out_specs=pl.BlockSpec(memory_space=pltpu.VMEM),
        scratch_shapes=[
            pltpu.VMEM(shape, signed_slab.dtype),
            pltpu.SemaphoreType.DMA((span, 3)),
            pltpu.SemaphoreType.DMA((pieces, lax.axis_size("win"), 3)),
            pltpu.SemaphoreType.DMA,
        ],
        compiler_params=pltpu.CompilerParams(collective_id=0, has_side_effects=True),
    )(cut)
    return held


def gelu(value):
    half = 0.5 * value
    inner = value * (0.7978845608028654 + 0.035677408136300125 * (value * value))
    return half + half * jnp.tanh(inner)


def network_kernel(rows, halo, layers, planes_ref, slabs_ref, mix_ref, out_ref, feats, depth):
    span, extended, commit, columns = planes_ref.shape
    rounds = span * commit
    channels = slabs_ref.shape[1]
    tail = 28 * layers
    gain_ref, bias_ref, read_ref = slabs_ref.at[tail], slabs_ref.at[tail + 1], slabs_ref.at[tail + 2]
    groups = channels // 8
    tiles = lax.axis_size("tile")
    first_row = lax.axis_index("tile") * rows - halo

    def inside(row):
        plane_row = first_row + row
        return (plane_row >= 0) & (plane_row < rows * tiles)

    def embed(row, carry):
        keep = inside(row)
        for t in range(rounds):
            plane = planes_ref[t // commit, row, pl.ds(t % commit, 1), :].astype(jnp.float32)
            value = plane * gain_ref[...] + bias_ref[...]
            value = value.astype(jnp.bfloat16).astype(jnp.float32)
            feats[0, row, :, pl.ds(t * columns, columns)] = jnp.where(keep, value, 0.0)
        return carry

    lax.fori_loop(0, extended, embed, 0)

    def spread(value):
        return (pltpu.roll(value, 1, 1), value, pltpu.roll(value, columns - 1, 1))

    for layer in range(layers):
        src, dst = layer % 2, (layer + 1) % 2
        last = layer == layers - 1

        def one_row(row, carry, layer=layer, src=src, dst=dst, last=last):
            def one_group(group, inner):
                lanes8 = pl.ds(pl.multiple_of(group * 8, 8), 8)
                weights = [slabs_ref[27 * layer + tap, lanes8, :] for tap in range(27)]
                running = {}
                for source in range(rounds):
                    cut = pl.ds(source * columns, columns)
                    held = [spread(feats[src, row - 1 + b, lanes8, cut]) for b in range(3)]
                    for a in range(3):
                        t = source - a + 1
                        if t < 0 or t >= rounds:
                            continue
                        for b in range(3):
                            for e in range(3):
                                term = weights[9 * a + 3 * b + e] * held[b][e]
                                running[t] = term if t not in running else running[t] + term
                    done = source - 1 if source < rounds - 1 else None
                    for t in ([done] if done is not None else [rounds - 2, rounds - 1]):
                        if t >= 0:
                            depth[lanes8, pl.ds(t * columns, columns)] = running.pop(t)
                return inner

            lax.fori_loop(0, groups, one_group, 0, unroll=8)
            mixed = jnp.dot(
                mix_ref[layer], depth[...].astype(jnp.bfloat16), preferred_element_type=jnp.float32
            )
            keep = inside(row)
            sums = []
            for t in range(rounds):
                cut = pl.ds(t * columns, columns)
                activated = gelu(mixed[:, t * columns : (t + 1) * columns] + slabs_ref[27 * layers + layer])
                value = (feats[src, row, :, cut] + activated).astype(jnp.bfloat16).astype(jnp.float32)
                value = jnp.where(keep, value, 0.0)
                if last:
                    sums.append(jnp.sum(value * read_ref[...], axis=0, keepdims=True))
                else:
                    feats[dst, row, :, cut] = value
            if last:
                out_ref[row - halo] = jnp.concatenate(sums, axis=0)
            return carry

        lax.fori_loop(layer + 1, extended - layer - 1, one_row, 0)


def run_network(planes, embed_gain, embed_bias, depth_kernel, point_weight, point_bias, read_weight, rows, halo):
    span, extended, commit, columns = planes.shape
    rounds = span * commit
    layers, channels, _ = depth_kernel.shape
    stacked = jnp.concatenate(
        [
            jnp.transpose(depth_kernel, (0, 2, 1)).reshape(-1, channels),
            point_bias,
            embed_gain[None],
            embed_bias[None],
            read_weight.astype(jnp.float32)[None],
        ],
        axis=0,
    )
    slabs = jnp.broadcast_to(stacked[..., None], stacked.shape + (columns,))
    lane = jnp.arange(columns)
    side = jnp.arange(stacked.shape[0]) % 3
    tap_rows = jnp.arange(stacked.shape[0]) < 27 * layers
    cancel = tap_rows[:, None] & (((side[:, None] == 0) & (lane == 0)) | ((side[:, None] == 2) & (lane == columns - 1)))
    slabs = jnp.where(cancel[:, None, :], 0.0, slabs)
    mix = jnp.transpose(point_weight, (0, 2, 1)).astype(jnp.bfloat16)
    vmem = pl.BlockSpec(memory_space=pltpu.VMEM)
    return pl.pallas_call(
        functools.partial(network_kernel, rows, halo, layers),
        out_shape=jax.ShapeDtypeStruct((rows, rounds, columns), jnp.float32),
        in_specs=[vmem] * 3,
        out_specs=vmem,
        scratch_shapes=[
            pltpu.VMEM((2, extended, channels, rounds * columns), jnp.float32),
            pltpu.VMEM((channels, rounds * columns), jnp.float32),
        ],
        compiler_params=pltpu.CompilerParams(vmem_limit_bytes=56 * 1024 * 1024),
    )(planes, slabs, mix)


def shards(
    axis_names,
    syndromes,
    confidence,
    embed_gain,
    embed_bias,
    depth_kernel,
    point_weight,
    point_bias,
    read_weight,
):
    layers = depth_kernel.shape[0]
    rows = syndromes.shape[1]
    signed_slab = ((2 * syndromes - 1).astype(jnp.float32) * confidence).astype(jnp.bfloat16)
    planes = gather_window(signed_slab, layers, axis_names)
    logits = run_network(
        planes, embed_gain, embed_bias, depth_kernel, point_weight, point_bias, read_weight, rows, layers
    )
    return jnp.transpose(logits, (1, 0, 2))[None]


def solution(mesh):
    placed = (P("win", "tile", None), P("win", "tile", None), P(), P(), P(), P(), P(), P())
    return jax.shard_map(
        functools.partial(shards, tuple(mesh.axis_names)), mesh=mesh, in_specs=placed, out_specs=P("win", None, "tile", None), check_vma=False
    )
```

```python
import functools

import jax
import jax.numpy as jnp
from jax import lax
from jax.experimental import pallas as pl
from jax.experimental.pallas import tpu as pltpu
from jax.sharding import PartitionSpec as P

WINDOW = 16
COMMIT = 2


def exchange_kernel(axis_names, halo, slab_ref, out_ref, held, recv_sem, send_sem, local_sem):
    tiles, wins = lax.axis_size("tile"), lax.axis_size("win")
    tile, win = lax.axis_index("tile"), lax.axis_index("win")
    pieces, rows = slab_ref.shape[0], slab_ref.shape[1]
    span = held.shape[0]

    def device(tile_index, win_index):
        place = {"tile": tile_index, "win": win_index}
        return tuple(place[name] for name in axis_names)

    mesh_ids = pl.DeviceIdType.MESH
    blank = jnp.zeros((span, halo) + held.shape[2:], held.dtype)

    @pl.when(tile == 0)
    def _():
        held[:, pl.ds(0, halo)] = blank

    @pl.when(tile == tiles - 1)
    def _():
        held[:, pl.ds(rows + halo, halo)] = blank

    neighbour_tiles = 1 + (tile > 0).astype(jnp.int32) + (tile < tiles - 1).astype(jnp.int32)
    barrier = pltpu.get_barrier_semaphore()
    for shift in (-1, 0, 1):
        for other in range(wins):
            there = tile + shift
            partner = (there >= 0) & (there < tiles)
            if shift == 0:
                partner = partner & (win != other)

            @pl.when(partner)
            def _():
                pl.semaphore_signal(barrier, 1, device_id=device(there, other), device_id_type=mesh_ids)

    pl.semaphore_wait(barrier, neighbour_tiles * wins - 1)

    parts = ((-1, 0, rows + halo, halo, 0), (0, 0, halo, rows, 1), (1, rows - halo, 0, halo, 0))
    started = []
    for piece in range(pieces):
        global_piece = win * pieces + piece
        for other in range(wins):
            offset = global_piece - other
            needed = (offset >= 0) & (offset < span)
            offset = jnp.clip(offset, 0, span - 1)
            for shift, src_row, dst_row, count, kind in parts:
                there = tile + shift
                ok = needed & (there >= 0) & (there < tiles)
                there = jnp.clip(there, 0, tiles - 1)
                src = slab_ref.at[pl.ds(piece, 1), pl.ds(src_row, count)]
                dst = held.at[pl.ds(offset, 1), pl.ds(dst_row, count)]
                if shift == 0:
                    local = ok & (win == other)
                    remote = ok & (win != other)
                    copy_local = pltpu.make_async_copy(src, dst, local_sem)

                    @pl.when(local)
                    def _():
                        copy_local.start()
                        copy_local.wait()
                else:
                    remote = ok
                copy = pltpu.make_async_remote_copy(
                    src_ref=src,
                    dst_ref=dst,
                    send_sem=send_sem.at[piece, other, shift + 1],
                    recv_sem=recv_sem.at[offset, shift + 1],
                    device_id=device(there, other),
                    device_id_type=mesh_ids,
                )

                @pl.when(remote)
                def _():
                    copy.start()

                started.append((remote, copy))

    for remote, copy in started:

        @pl.when(remote)
        def _():
            copy.wait_send()

    for step in range(span):
        source_win = (win + step) // pieces
        for shift, src_row, dst_row, count, kind in parts:
            there = tile - shift
            ok = (there >= 0) & (there < tiles)
            if shift == 0:
                ok = ok & (source_win != win)
            probe = pltpu.make_async_remote_copy(
                src_ref=slab_ref.at[pl.ds(0, 1), pl.ds(src_row, count)],
                dst_ref=held.at[pl.ds(0, 1), pl.ds(dst_row, count)],
                send_sem=send_sem.at[0, 0, shift + 1],
                recv_sem=recv_sem.at[step, shift + 1],
                device_id=device(there, win),
                device_id_type=mesh_ids,
            )

            @pl.when(ok)
            def _():
                probe.wait_recv()

    out_ref[...] = held[...]


def gather_window(signed_slab, halo, axis_names):
    rounds, rows, columns = signed_slab.shape
    pieces = rounds // COMMIT
    span = WINDOW // COMMIT
    cut = jnp.transpose(signed_slab.reshape(pieces, COMMIT, rows, columns), (0, 2, 1, 3))
    shape = (span, rows + 2 * halo, COMMIT, columns)
    held = pl.pallas_call(
        functools.partial(exchange_kernel, axis_names, halo),
        out_shape=jax.ShapeDtypeStruct(shape, signed_slab.dtype),
        in_specs=[pl.BlockSpec(memory_space=pltpu.VMEM)],
        out_specs=pl.BlockSpec(memory_space=pltpu.VMEM),
        scratch_shapes=[
            pltpu.VMEM(shape, signed_slab.dtype),
            pltpu.SemaphoreType.DMA((span, 3)),
            pltpu.SemaphoreType.DMA((pieces, lax.axis_size("win"), 3)),
            pltpu.SemaphoreType.DMA,
        ],
        compiler_params=pltpu.CompilerParams(collective_id=0, has_side_effects=True),
    )(cut)
    return held


def gelu(value):
    half = 0.5 * value
    inner = value * (0.7978845608028654 + 0.035677408136300125 * (value * value))
    return half + half * jnp.tanh(inner)


def network_kernel(rows, halo, layers, planes_ref, slabs_ref, mix_ref, out_ref, feats, depth):
    span, extended, commit, columns = planes_ref.shape
    rounds = span * commit
    channels = slabs_ref.shape[1]
    tail = 28 * layers
    gain_ref, bias_ref, read_ref = slabs_ref.at[tail], slabs_ref.at[tail + 1], slabs_ref.at[tail + 2]
    groups = channels // 8
    tiles = lax.axis_size("tile")
    first_row = lax.axis_index("tile") * rows - halo

    def inside(row):
        plane_row = first_row + row
        return (plane_row >= 0) & (plane_row < rows * tiles)

    def embed(row, carry):
        keep = inside(row)
        for t in range(rounds):
            plane = planes_ref[t // commit, row, pl.ds(t % commit, 1), :].astype(jnp.float32)
            value = plane * gain_ref[...] + bias_ref[...]
            value = value.astype(jnp.bfloat16).astype(jnp.float32)
            feats[0, row, :, pl.ds(t * columns, columns)] = jnp.where(keep, value, 0.0)
        return carry

    lax.fori_loop(0, extended, embed, 0)

    def spread(value):
        return (pltpu.roll(value, 1, 1), value, pltpu.roll(value, columns - 1, 1))

    for layer in range(layers):
        src, dst = layer % 2, (layer + 1) % 2
        last = layer == layers - 1

        def one_row(row, carry, layer=layer, src=src, dst=dst, last=last):
            def one_group(group, inner):
                lanes8 = pl.ds(pl.multiple_of(group * 8, 8), 8)
                weights = [slabs_ref[27 * layer + tap, lanes8, :] for tap in range(27)]
                running = {}
                for source in range(rounds):
                    cut = pl.ds(source * columns, columns)
                    held = [spread(feats[src, row - 1 + b, lanes8, cut]) for b in range(3)]
                    for a in range(3):
                        t = source - a + 1
                        if t < 0 or t >= rounds:
                            continue
                        for b in range(3):
                            for e in range(3):
                                term = weights[9 * a + 3 * b + e] * held[b][e]
                                running[t] = term if t not in running else running[t] + term
                    done = source - 1 if source < rounds - 1 else None
                    for t in ([done] if done is not None else [rounds - 2, rounds - 1]):
                        if t >= 0:
                            depth[lanes8, pl.ds(t * columns, columns)] = running.pop(t)
                return inner

            lax.fori_loop(0, groups, one_group, 0, unroll=8)
            mixed = jnp.dot(
                mix_ref[layer], depth[...].astype(jnp.bfloat16), preferred_element_type=jnp.float32
            )
            keep = inside(row)
            sums = []
            for t in range(rounds):
                cut = pl.ds(t * columns, columns)
                activated = gelu(mixed[:, t * columns : (t + 1) * columns] + slabs_ref[27 * layers + layer])
                value = (feats[src, row, :, cut] + activated).astype(jnp.bfloat16).astype(jnp.float32)
                value = jnp.where(keep, value, 0.0)
                if last:
                    sums.append(jnp.sum(value * read_ref[...], axis=0, keepdims=True))
                else:
                    feats[dst, row, :, cut] = value
            if last:
                for t in range(rounds):
                    out_ref[t, pl.ds(row - halo, 1), :] = sums[t]
            return carry

        lax.fori_loop(layer + 1, extended - layer - 1, one_row, 0)


def run_network(planes, embed_gain, embed_bias, depth_kernel, point_weight, point_bias, read_weight, rows, halo):
    span, extended, commit, columns = planes.shape
    rounds = span * commit
    layers, channels, _ = depth_kernel.shape
    stacked = jnp.concatenate(
        [
            jnp.transpose(depth_kernel, (0, 2, 1)).reshape(-1, channels),
            point_bias,
            embed_gain[None],
            embed_bias[None],
            read_weight.astype(jnp.float32)[None],
        ],
        axis=0,
    )
    slabs = jnp.broadcast_to(stacked[..., None], stacked.shape + (columns,))
    lane = jnp.arange(columns)
    side = jnp.arange(stacked.shape[0]) % 3
    tap_rows = jnp.arange(stacked.shape[0]) < 27 * layers
    cancel = tap_rows[:, None] & (((side[:, None] == 0) & (lane == 0)) | ((side[:, None] == 2) & (lane == columns - 1)))
    slabs = jnp.where(cancel[:, None, :], 0.0, slabs)
    mix = jnp.transpose(point_weight, (0, 2, 1)).astype(jnp.bfloat16)
    vmem = pl.BlockSpec(memory_space=pltpu.VMEM)
    return pl.pallas_call(
        functools.partial(network_kernel, rows, halo, layers),
        out_shape=jax.ShapeDtypeStruct((rounds, rows, columns), jnp.float32),
        in_specs=[vmem] * 3,
        out_specs=vmem,
        scratch_shapes=[
            pltpu.VMEM((2, extended, channels, rounds * columns), jnp.float32),
            pltpu.VMEM((channels, rounds * columns), jnp.float32),
        ],
        compiler_params=pltpu.CompilerParams(vmem_limit_bytes=56 * 1024 * 1024),
    )(planes, slabs, mix)


def shards(
    axis_names,
    syndromes,
    confidence,
    embed_gain,
    embed_bias,
    depth_kernel,
    point_weight,
    point_bias,
    read_weight,
):
    layers = depth_kernel.shape[0]
    rows = syndromes.shape[1]
    signed_slab = ((2 * syndromes - 1).astype(jnp.float32) * confidence).astype(jnp.bfloat16)
    planes = gather_window(signed_slab, layers, axis_names)
    logits = run_network(
        planes, embed_gain, embed_bias, depth_kernel, point_weight, point_bias, read_weight, rows, layers
    )
    return logits[None]


def solution(mesh):
    placed = (P("win", "tile", None), P("win", "tile", None), P(), P(), P(), P(), P(), P())
    return jax.shard_map(
        functools.partial(shards, tuple(mesh.axis_names)), mesh=mesh, in_specs=placed, out_specs=P("win", None, "tile", None), check_vma=False
    )
```

```python
import functools

import jax
import jax.numpy as jnp
from jax import lax
from jax.experimental import pallas as pl
from jax.experimental.pallas import tpu as pltpu
from jax.sharding import PartitionSpec as P

WINDOW = 16
COMMIT = 2


def exchange_kernel(axis_names, halo, slab_ref, out_ref, held, recv_sem, send_sem, local_sem):
    tiles, wins = lax.axis_size("tile"), lax.axis_size("win")
    tile, win = lax.axis_index("tile"), lax.axis_index("win")
    pieces, rows = slab_ref.shape[0], slab_ref.shape[1]
    span = held.shape[0]

    def device(tile_index, win_index):
        place = {"tile": tile_index, "win": win_index}
        return tuple(place[name] for name in axis_names)

    mesh_ids = pl.DeviceIdType.MESH
    blank = jnp.zeros((span, halo) + held.shape[2:], held.dtype)

    @pl.when(tile == 0)
    def _():
        held[:, pl.ds(0, halo)] = blank

    @pl.when(tile == tiles - 1)
    def _():
        held[:, pl.ds(rows + halo, halo)] = blank

    neighbour_tiles = 1 + (tile > 0).astype(jnp.int32) + (tile < tiles - 1).astype(jnp.int32)
    barrier = pltpu.get_barrier_semaphore()
    for shift in (-1, 0, 1):
        for other in range(wins):
            there = tile + shift
            partner = (there >= 0) & (there < tiles)
            if shift == 0:
                partner = partner & (win != other)

            @pl.when(partner)
            def _():
                pl.semaphore_signal(barrier, 1, device_id=device(there, other), device_id_type=mesh_ids)

    pl.semaphore_wait(barrier, neighbour_tiles * wins - 1)

    parts = ((-1, 0, rows + halo, halo, 0), (0, 0, halo, rows, 1), (1, rows - halo, 0, halo, 0))
    started = []
    for piece in range(pieces):
        global_piece = win * pieces + piece
        for other in range(wins):
            offset = global_piece - other
            needed = (offset >= 0) & (offset < span)
            offset = jnp.clip(offset, 0, span - 1)
            for shift, src_row, dst_row, count, kind in parts:
                there = tile + shift
                ok = needed & (there >= 0) & (there < tiles)
                there = jnp.clip(there, 0, tiles - 1)
                src = slab_ref.at[pl.ds(piece, 1), pl.ds(src_row, count)]
                dst = held.at[pl.ds(offset, 1), pl.ds(dst_row, count)]
                if shift == 0:
                    local = ok & (win == other)
                    remote = ok & (win != other)
                    copy_local = pltpu.make_async_copy(src, dst, local_sem)

                    @pl.when(local)
                    def _():
                        copy_local.start()
                        copy_local.wait()
                else:
                    remote = ok
                copy = pltpu.make_async_remote_copy(
                    src_ref=src,
                    dst_ref=dst,
                    send_sem=send_sem.at[piece, other, shift + 1],
                    recv_sem=recv_sem.at[offset, shift + 1],
                    device_id=device(there, other),
                    device_id_type=mesh_ids,
                )

                @pl.when(remote)
                def _():
                    copy.start()

                started.append((remote, copy))

    for remote, copy in started:

        @pl.when(remote)
        def _():
            copy.wait_send()

    for step in range(span):
        source_win = (win + step) // pieces
        for shift, src_row, dst_row, count, kind in parts:
            there = tile - shift
            ok = (there >= 0) & (there < tiles)
            if shift == 0:
                ok = ok & (source_win != win)
            probe = pltpu.make_async_remote_copy(
                src_ref=slab_ref.at[pl.ds(0, 1), pl.ds(src_row, count)],
                dst_ref=held.at[pl.ds(0, 1), pl.ds(dst_row, count)],
                send_sem=send_sem.at[0, 0, shift + 1],
                recv_sem=recv_sem.at[step, shift + 1],
                device_id=device(there, win),
                device_id_type=mesh_ids,
            )

            @pl.when(ok)
            def _():
                probe.wait_recv()

    out_ref[...] = held[...]


def gather_window(signed_slab, halo, axis_names):
    rounds, rows, columns = signed_slab.shape
    pieces = rounds // COMMIT
    span = WINDOW // COMMIT
    cut = jnp.transpose(signed_slab.reshape(pieces, COMMIT, rows, columns), (0, 2, 1, 3))
    shape = (span, rows + 2 * halo, COMMIT, columns)
    held = pl.pallas_call(
        functools.partial(exchange_kernel, axis_names, halo),
        out_shape=jax.ShapeDtypeStruct(shape, signed_slab.dtype),
        in_specs=[pl.BlockSpec(memory_space=pltpu.VMEM)],
        out_specs=pl.BlockSpec(memory_space=pltpu.VMEM),
        scratch_shapes=[
            pltpu.VMEM(shape, signed_slab.dtype),
            pltpu.SemaphoreType.DMA((span, 3)),
            pltpu.SemaphoreType.DMA((pieces, lax.axis_size("win"), 3)),
            pltpu.SemaphoreType.DMA,
        ],
        compiler_params=pltpu.CompilerParams(collective_id=0, has_side_effects=True),
    )(cut)
    return held


def gelu(value):
    half = 0.5 * value
    inner = value * (0.7978845608028654 + 0.035677408136300125 * (value * value))
    return half + half * jnp.tanh(inner)


def network_kernel(rows, halo, layers, planes_ref, slabs_ref, mix_ref, out_ref, feats, depth):
    span, extended, commit, columns = planes_ref.shape
    rounds = span * commit
    channels = slabs_ref.shape[1]
    tail = 28 * layers
    gain_ref, bias_ref, read_ref = slabs_ref.at[tail], slabs_ref.at[tail + 1], slabs_ref.at[tail + 2]
    groups = channels // 8
    tiles = lax.axis_size("tile")
    first_row = lax.axis_index("tile") * rows - halo

    def inside(row):
        plane_row = first_row + row
        return (plane_row >= 0) & (plane_row < rows * tiles)

    def embed(row, carry):
        keep = inside(row)
        for t in range(rounds):
            plane = planes_ref[t // commit, row, pl.ds(t % commit, 1), :].astype(jnp.float32)
            value = plane * gain_ref[...] + bias_ref[...]
            value = value.astype(jnp.bfloat16).astype(jnp.float32)
            feats[0, row, :, pl.ds(t * columns, columns)] = jnp.where(keep, value, 0.0)
        return carry

    lax.fori_loop(0, extended, embed, 0)

    def spread(value):
        return (pltpu.roll(value, 1, 1), value, pltpu.roll(value, columns - 1, 1))

    for layer in range(layers):
        src, dst = layer % 2, (layer + 1) % 2
        last = layer == layers - 1

        def one_row(row, carry, layer=layer, src=src, dst=dst, last=last):
            def one_group(group, inner):
                lanes8 = pl.ds(pl.multiple_of(group * 8, 8), 8)
                weights = [slabs_ref[27 * layer + tap, lanes8, :] for tap in range(27)]
                running = {}
                for source in range(rounds):
                    cut = pl.ds(source * columns, columns)
                    held = [spread(feats[src, row - 1 + b, lanes8, cut]) for b in range(3)]
                    for a in range(3):
                        t = source - a + 1
                        if t < 0 or t >= rounds:
                            continue
                        for b in range(3):
                            for e in range(3):
                                term = weights[9 * a + 3 * b + e] * held[b][e]
                                running[t] = term if t not in running else running[t] + term
                    done = source - 1 if source < rounds - 1 else None
                    for t in ([done] if done is not None else [rounds - 2, rounds - 1]):
                        if t >= 0:
                            depth[lanes8, pl.ds(t * columns, columns)] = running.pop(t)
                return inner

            lax.fori_loop(0, groups, one_group, 0, unroll=8)
            mixed = lax.dot_general(
                mix_ref[layer],
                depth[...].astype(jnp.bfloat16),
                (((0,), (0,)), ((), ())),
                preferred_element_type=jnp.float32,
            )
            keep = inside(row)
            sums = []
            for t in range(rounds):
                cut = pl.ds(t * columns, columns)
                activated = gelu(mixed[:, t * columns : (t + 1) * columns] + slabs_ref[27 * layers + layer])
                value = (feats[src, row, :, cut] + activated).astype(jnp.bfloat16).astype(jnp.float32)
                value = jnp.where(keep, value, 0.0)
                if last:
                    sums.append(jnp.sum(value * read_ref[...], axis=0, keepdims=True))
                else:
                    feats[dst, row, :, cut] = value
            if last:
                for t in range(rounds):
                    out_ref[t, pl.ds(row - halo, 1), :] = sums[t]
            return carry

        lax.fori_loop(layer + 1, extended - layer - 1, one_row, 0)


def run_network(planes, embed_gain, embed_bias, depth_kernel, point_weight, point_bias, read_weight, rows, halo):
    span, extended, commit, columns = planes.shape
    rounds = span * commit
    layers, channels, _ = depth_kernel.shape
    stacked = jnp.concatenate(
        [
            jnp.transpose(depth_kernel, (0, 2, 1)).reshape(-1, channels),
            point_bias,
            embed_gain[None],
            embed_bias[None],
            read_weight.astype(jnp.float32)[None],
        ],
        axis=0,
    )
    slabs = jnp.broadcast_to(stacked[..., None], stacked.shape + (columns,))
    lane = jnp.arange(columns)
    side = jnp.arange(stacked.shape[0]) % 3
    tap_rows = jnp.arange(stacked.shape[0]) < 27 * layers
    cancel = tap_rows[:, None] & (((side[:, None] == 0) & (lane == 0)) | ((side[:, None] == 2) & (lane == columns - 1)))
    slabs = jnp.where(cancel[:, None, :], 0.0, slabs)
    mix = point_weight.astype(jnp.bfloat16)
    vmem = pl.BlockSpec(memory_space=pltpu.VMEM)
    return pl.pallas_call(
        functools.partial(network_kernel, rows, halo, layers),
        out_shape=jax.ShapeDtypeStruct((rounds, rows, columns), jnp.float32),
        in_specs=[vmem] * 3,
        out_specs=vmem,
        scratch_shapes=[
            pltpu.VMEM((2, extended, channels, rounds * columns), jnp.float32),
            pltpu.VMEM((channels, rounds * columns), jnp.float32),
        ],
        compiler_params=pltpu.CompilerParams(vmem_limit_bytes=56 * 1024 * 1024),
    )(planes, slabs, mix)


def shards(
    axis_names,
    syndromes,
    confidence,
    embed_gain,
    embed_bias,
    depth_kernel,
    point_weight,
    point_bias,
    read_weight,
):
    layers = depth_kernel.shape[0]
    rows = syndromes.shape[1]
    signed_slab = ((2 * syndromes - 1).astype(jnp.float32) * confidence).astype(jnp.bfloat16)
    planes = gather_window(signed_slab, layers, axis_names)
    logits = run_network(
        planes, embed_gain, embed_bias, depth_kernel, point_weight, point_bias, read_weight, rows, layers
    )
    return logits[None]


def solution(mesh):
    placed = (P("win", "tile", None), P("win", "tile", None), P(), P(), P(), P(), P(), P())
    return jax.shard_map(
        functools.partial(shards, tuple(mesh.axis_names)), mesh=mesh, in_specs=placed, out_specs=P("win", None, "tile", None), check_vma=False
    )
```

```python
import functools

import jax
import jax.numpy as jnp
from jax import lax
from jax.experimental import pallas as pl
from jax.experimental.pallas import tpu as pltpu
from jax.sharding import PartitionSpec as P

WINDOW = 16
COMMIT = 2


def exchange_kernel(axis_names, halo, slab_ref, out_ref, held, recv_sem, send_sem, local_sem):
    tiles, wins = lax.axis_size("tile"), lax.axis_size("win")
    tile, win = lax.axis_index("tile"), lax.axis_index("win")
    pieces, rows = slab_ref.shape[0], slab_ref.shape[1]
    span = held.shape[0]

    def device(tile_index, win_index):
        place = {"tile": tile_index, "win": win_index}
        return tuple(place[name] for name in axis_names)

    mesh_ids = pl.DeviceIdType.MESH
    blank = jnp.zeros((span, halo) + held.shape[2:], held.dtype)

    @pl.when(tile == 0)
    def _():
        held[:, pl.ds(0, halo)] = blank

    @pl.when(tile == tiles - 1)
    def _():
        held[:, pl.ds(rows + halo, halo)] = blank

    neighbour_tiles = 1 + (tile > 0).astype(jnp.int32) + (tile < tiles - 1).astype(jnp.int32)

    def linked(other):
        sends = (other >= win * pieces - span + 1) & (other <= win * pieces + pieces - 1)
        takes = (other * pieces <= win + span - 1) & ((other + 1) * pieces - 1 >= win)
        return sends | takes

    linked_wins = sum(linked(other).astype(jnp.int32) for other in range(wins))
    barrier = pltpu.get_barrier_semaphore()
    for shift in (-1, 0, 1):
        for other in range(wins):
            there = tile + shift
            partner = (there >= 0) & (there < tiles) & linked(other)
            if shift == 0:
                partner = partner & (win != other)

            @pl.when(partner)
            def _():
                pl.semaphore_signal(barrier, 1, device_id=device(there, other), device_id_type=mesh_ids)

    pl.semaphore_wait(barrier, neighbour_tiles * linked_wins - 1)

    parts = ((-1, 0, rows + halo, halo, 0), (0, 0, halo, rows, 1), (1, rows - halo, 0, halo, 0))
    started = []
    for piece in range(pieces):
        global_piece = win * pieces + piece
        for other in range(wins):
            offset = global_piece - other
            needed = (offset >= 0) & (offset < span)
            offset = jnp.clip(offset, 0, span - 1)
            for shift, src_row, dst_row, count, kind in parts:
                there = tile + shift
                ok = needed & (there >= 0) & (there < tiles)
                there = jnp.clip(there, 0, tiles - 1)
                src = slab_ref.at[pl.ds(piece, 1), pl.ds(src_row, count)]
                dst = held.at[pl.ds(offset, 1), pl.ds(dst_row, count)]
                if shift == 0:
                    local = ok & (win == other)
                    remote = ok & (win != other)
                    copy_local = pltpu.make_async_copy(src, dst, local_sem)

                    @pl.when(local)
                    def _():
                        copy_local.start()
                        copy_local.wait()
                else:
                    remote = ok
                copy = pltpu.make_async_remote_copy(
                    src_ref=src,
                    dst_ref=dst,
                    send_sem=send_sem.at[piece, other, shift + 1],
                    recv_sem=recv_sem.at[offset, shift + 1],
                    device_id=device(there, other),
                    device_id_type=mesh_ids,
                )

                @pl.when(remote)
                def _():
                    copy.start()

                started.append((remote, copy))

    for remote, copy in started:

        @pl.when(remote)
        def _():
            copy.wait_send()

    for step in range(span):
        source_win = (win + step) // pieces
        for shift, src_row, dst_row, count, kind in parts:
            there = tile - shift
            ok = (there >= 0) & (there < tiles)
            if shift == 0:
                ok = ok & (source_win != win)
            probe = pltpu.make_async_remote_copy(
                src_ref=slab_ref.at[pl.ds(0, 1), pl.ds(src_row, count)],
                dst_ref=held.at[pl.ds(0, 1), pl.ds(dst_row, count)],
                send_sem=send_sem.at[0, 0, shift + 1],
                recv_sem=recv_sem.at[step, shift + 1],
                device_id=device(there, win),
                device_id_type=mesh_ids,
            )

            @pl.when(ok)
            def _():
                probe.wait_recv()

    out_ref[...] = held[...]


def gather_window(signed_slab, halo, axis_names):
    rounds, rows, columns = signed_slab.shape
    pieces = rounds // COMMIT
    span = WINDOW // COMMIT
    cut = jnp.transpose(signed_slab.reshape(pieces, COMMIT, rows, columns), (0, 2, 1, 3))
    shape = (span, rows + 2 * halo, COMMIT, columns)
    held = pl.pallas_call(
        functools.partial(exchange_kernel, axis_names, halo),
        out_shape=jax.ShapeDtypeStruct(shape, signed_slab.dtype),
        in_specs=[pl.BlockSpec(memory_space=pltpu.VMEM)],
        out_specs=pl.BlockSpec(memory_space=pltpu.VMEM),
        scratch_shapes=[
            pltpu.VMEM(shape, signed_slab.dtype),
            pltpu.SemaphoreType.DMA((span, 3)),
            pltpu.SemaphoreType.DMA((pieces, lax.axis_size("win"), 3)),
            pltpu.SemaphoreType.DMA,
        ],
        compiler_params=pltpu.CompilerParams(collective_id=0, has_side_effects=True),
    )(cut)
    return held


def gelu(value):
    half = 0.5 * value
    inner = value * (0.7978845608028654 + 0.035677408136300125 * (value * value))
    return half + half * jnp.tanh(inner)


def network_kernel(rows, halo, layers, planes_ref, slabs_ref, mix_ref, out_ref, feats, depth):
    span, extended, commit, columns = planes_ref.shape
    rounds = span * commit
    channels = slabs_ref.shape[1]
    tail = 28 * layers
    gain_ref, bias_ref, read_ref = slabs_ref.at[tail], slabs_ref.at[tail + 1], slabs_ref.at[tail + 2]
    groups = channels // 8
    tiles = lax.axis_size("tile")
    first_row = lax.axis_index("tile") * rows - halo

    def inside(row):
        plane_row = first_row + row
        return (plane_row >= 0) & (plane_row < rows * tiles)

    def embed(row, carry):
        keep = inside(row)
        for t in range(rounds):
            plane = planes_ref[t // commit, row, pl.ds(t % commit, 1), :].astype(jnp.float32)
            value = plane * gain_ref[...] + bias_ref[...]
            value = value.astype(jnp.bfloat16).astype(jnp.float32)
            feats[0, row, :, pl.ds(t * columns, columns)] = jnp.where(keep, value, 0.0)
        return carry

    lax.fori_loop(0, extended, embed, 0)

    def spread(value):
        return (pltpu.roll(value, 1, 1), value, pltpu.roll(value, columns - 1, 1))

    for layer in range(layers):
        src, dst = layer % 2, (layer + 1) % 2
        last = layer == layers - 1

        def one_row(row, carry, layer=layer, src=src, dst=dst, last=last):
            def one_group(group, inner):
                lanes8 = pl.ds(pl.multiple_of(group * 8, 8), 8)
                weights = [slabs_ref[27 * layer + tap, lanes8, :] for tap in range(27)]
                running = {}
                for source in range(rounds):
                    cut = pl.ds(source * columns, columns)
                    held = [spread(feats[src, row - 1 + b, lanes8, cut]) for b in range(3)]
                    for a in range(3):
                        t = source - a + 1
                        if t < 0 or t >= rounds:
                            continue
                        for b in range(3):
                            for e in range(3):
                                term = weights[9 * a + 3 * b + e] * held[b][e]
                                running[t] = term if t not in running else running[t] + term
                    done = source - 1 if source < rounds - 1 else None
                    for t in ([done] if done is not None else [rounds - 2, rounds - 1]):
                        if t >= 0:
                            depth[lanes8, pl.ds(t * columns, columns)] = running.pop(t)
                return inner

            lax.fori_loop(0, groups, one_group, 0, unroll=8)
            mixed = jnp.dot(
                mix_ref[layer], depth[...].astype(jnp.bfloat16), preferred_element_type=jnp.float32
            )
            keep = inside(row)
            sums = []
            for t in range(rounds):
                cut = pl.ds(t * columns, columns)
                activated = gelu(mixed[:, t * columns : (t + 1) * columns] + slabs_ref[27 * layers + layer])
                value = (feats[src, row, :, cut] + activated).astype(jnp.bfloat16).astype(jnp.float32)
                value = jnp.where(keep, value, 0.0)
                if last:
                    sums.append(jnp.sum(value * read_ref[...], axis=0, keepdims=True))
                else:
                    feats[dst, row, :, cut] = value
            if last:
                for t in range(rounds):
                    out_ref[t, pl.ds(row - halo, 1), :] = sums[t]
            return carry

        lax.fori_loop(layer + 1, extended - layer - 1, one_row, 0)


def run_network(planes, embed_gain, embed_bias, depth_kernel, point_weight, point_bias, read_weight, rows, halo):
    span, extended, commit, columns = planes.shape
    rounds = span * commit
    layers, channels, _ = depth_kernel.shape
    stacked = jnp.concatenate(
        [
            jnp.transpose(depth_kernel, (0, 2, 1)).reshape(-1, channels),
            point_bias,
            embed_gain[None],
            embed_bias[None],
            read_weight.astype(jnp.float32)[None],
        ],
        axis=0,
    )
    slabs = jnp.broadcast_to(stacked[..., None], stacked.shape + (columns,))
    lane = jnp.arange(columns)
    side = jnp.arange(stacked.shape[0]) % 3
    tap_rows = jnp.arange(stacked.shape[0]) < 27 * layers
    cancel = tap_rows[:, None] & (((side[:, None] == 0) & (lane == 0)) | ((side[:, None] == 2) & (lane == columns - 1)))
    slabs = jnp.where(cancel[:, None, :], 0.0, slabs)
    mix = jnp.transpose(point_weight, (0, 2, 1)).astype(jnp.bfloat16)
    vmem = pl.BlockSpec(memory_space=pltpu.VMEM)
    return pl.pallas_call(
        functools.partial(network_kernel, rows, halo, layers),
        out_shape=jax.ShapeDtypeStruct((rounds, rows, columns), jnp.float32),
        in_specs=[vmem] * 3,
        out_specs=vmem,
        scratch_shapes=[
            pltpu.VMEM((2, extended, channels, rounds * columns), jnp.float32),
            pltpu.VMEM((channels, rounds * columns), jnp.float32),
        ],
        compiler_params=pltpu.CompilerParams(vmem_limit_bytes=56 * 1024 * 1024),
    )(planes, slabs, mix)


def shards(
    axis_names,
    syndromes,
    confidence,
    embed_gain,
    embed_bias,
    depth_kernel,
    point_weight,
    point_bias,
    read_weight,
):
    layers = depth_kernel.shape[0]
    rows = syndromes.shape[1]
    signed_slab = ((2 * syndromes - 1).astype(jnp.float32) * confidence).astype(jnp.bfloat16)
    planes = gather_window(signed_slab, layers, axis_names)
    logits = run_network(
        planes, embed_gain, embed_bias, depth_kernel, point_weight, point_bias, read_weight, rows, layers
    )
    return logits[None]


def solution(mesh):
    placed = (P("win", "tile", None), P("win", "tile", None), P(), P(), P(), P(), P(), P())
    return jax.shard_map(
        functools.partial(shards, tuple(mesh.axis_names)), mesh=mesh, in_specs=placed, out_specs=P("win", None, "tile", None), check_vma=False
    )
```

```python
import functools

import jax
import jax.numpy as jnp
from jax import lax
from jax.experimental import pallas as pl
from jax.experimental.pallas import tpu as pltpu
from jax.sharding import PartitionSpec as P

WINDOW = 16
COMMIT = 2


def exchange_kernel(axis_names, halo, slab_ref, out_ref, held, recv_sem, send_sem, local_sem):
    tiles, wins = lax.axis_size("tile"), lax.axis_size("win")
    tile, win = lax.axis_index("tile"), lax.axis_index("win")
    pieces, rows = slab_ref.shape[0], slab_ref.shape[1]
    span = held.shape[0]

    def device(tile_index, win_index):
        place = {"tile": tile_index, "win": win_index}
        return tuple(place[name] for name in axis_names)

    mesh_ids = pl.DeviceIdType.MESH
    blank = jnp.zeros((span, halo) + held.shape[2:], held.dtype)

    @pl.when(tile == 0)
    def _():
        held[:, pl.ds(0, halo)] = blank

    @pl.when(tile == tiles - 1)
    def _():
        held[:, pl.ds(rows + halo, halo)] = blank

    neighbour_tiles = 1 + (tile > 0).astype(jnp.int32) + (tile < tiles - 1).astype(jnp.int32)
    barrier = pltpu.get_barrier_semaphore()
    for shift in (-1, 0, 1):
        for other in range(wins):
            there = tile + shift
            partner = (there >= 0) & (there < tiles)
            if shift == 0:
                partner = partner & (win != other)

            @pl.when(partner)
            def _():
                pl.semaphore_signal(barrier, 1, device_id=device(there, other), device_id_type=mesh_ids)

    pl.semaphore_wait(barrier, neighbour_tiles * wins - 1)

    parts = ((-1, 0, rows + halo, halo, 0), (0, 0, halo, rows, 1), (1, rows - halo, 0, halo, 0))
    started = []
    for piece in range(pieces):
        global_piece = win * pieces + piece
        for other in range(wins):
            offset = global_piece - other
            needed = (offset >= 0) & (offset < span)
            offset = jnp.clip(offset, 0, span - 1)
            for shift, src_row, dst_row, count, kind in parts:
                there = tile + shift
                ok = needed & (there >= 0) & (there < tiles)
                there = jnp.clip(there, 0, tiles - 1)
                src = slab_ref.at[pl.ds(piece, 1), pl.ds(src_row, count)]
                dst = held.at[pl.ds(offset, 1), pl.ds(dst_row, count)]
                if shift == 0:
                    local = ok & (win == other)
                    remote = ok & (win != other)
                    copy_local = pltpu.make_async_copy(src, dst, local_sem)

                    @pl.when(local)
                    def _():
                        copy_local.start()
                        copy_local.wait()
                else:
                    remote = ok
                copy = pltpu.make_async_remote_copy(
                    src_ref=src,
                    dst_ref=dst,
                    send_sem=send_sem.at[piece, other, shift + 1],
                    recv_sem=recv_sem.at[offset, shift + 1],
                    device_id=device(there, other),
                    device_id_type=mesh_ids,
                )

                @pl.when(remote)
                def _():
                    copy.start()

                started.append((remote, copy))

    for remote, copy in started:

        @pl.when(remote)
        def _():
            copy.wait_send()

    for step in range(span):
        source_win = (win + step) // pieces
        for shift, src_row, dst_row, count, kind in parts:
            there = tile - shift
            ok = (there >= 0) & (there < tiles)
            if shift == 0:
                ok = ok & (source_win != win)
            probe = pltpu.make_async_remote_copy(
                src_ref=slab_ref.at[pl.ds(0, 1), pl.ds(src_row, count)],
                dst_ref=held.at[pl.ds(0, 1), pl.ds(dst_row, count)],
                send_sem=send_sem.at[0, 0, shift + 1],
                recv_sem=recv_sem.at[step, shift + 1],
                device_id=device(there, win),
                device_id_type=mesh_ids,
            )

            @pl.when(ok)
            def _():
                probe.wait_recv()

    out_ref[...] = held[...]


def gather_window(signed_slab, halo, axis_names):
    rounds, rows, columns = signed_slab.shape
    pieces = rounds // COMMIT
    span = WINDOW // COMMIT
    cut = jnp.transpose(signed_slab.reshape(pieces, COMMIT, rows, columns), (0, 2, 1, 3))
    shape = (span, rows + 2 * halo, COMMIT, columns)
    held = pl.pallas_call(
        functools.partial(exchange_kernel, axis_names, halo),
        out_shape=jax.ShapeDtypeStruct(shape, signed_slab.dtype),
        in_specs=[pl.BlockSpec(memory_space=pltpu.VMEM)],
        out_specs=pl.BlockSpec(memory_space=pltpu.VMEM),
        scratch_shapes=[
            pltpu.VMEM(shape, signed_slab.dtype),
            pltpu.SemaphoreType.DMA((span, 3)),
            pltpu.SemaphoreType.DMA((pieces, lax.axis_size("win"), 3)),
            pltpu.SemaphoreType.DMA,
        ],
        compiler_params=pltpu.CompilerParams(collective_id=0, has_side_effects=True),
    )(cut)
    return held


def gelu(value):
    half = 0.5 * value
    inner = value * (0.7978845608028654 + 0.035677408136300125 * (value * value))
    return half + half * jnp.tanh(inner)


def network_kernel(rows, halo, layers, planes_ref, slabs_ref, small_ref, mix_ref, out_ref, feats, depth):
    span, extended, commit, columns = planes_ref.shape
    rounds = span * commit
    channels = slabs_ref.shape[1]
    gain_ref, bias_ref, read_ref = small_ref.at[0], small_ref.at[1], small_ref.at[2]
    groups = channels // 8
    tiles = lax.axis_size("tile")
    first_row = lax.axis_index("tile") * rows - halo

    def inside(row):
        plane_row = first_row + row
        return (plane_row >= 0) & (plane_row < rows * tiles)

    def embed(row, carry):
        keep = inside(row)
        for t in range(rounds):
            plane = planes_ref[t // commit, row, pl.ds(t % commit, 1), :].astype(jnp.float32)
            value = plane * gain_ref[...] + bias_ref[...]
            value = value.astype(jnp.bfloat16).astype(jnp.float32)
            feats[0, row, :, pl.ds(t * columns, columns)] = jnp.where(keep, value, 0.0)
        return carry

    lax.fori_loop(0, extended, embed, 0)

    def spread(value):
        return (pltpu.roll(value, 1, 1), value, pltpu.roll(value, columns - 1, 1))

    for layer in range(layers):
        src, dst = layer % 2, (layer + 1) % 2
        last = layer == layers - 1

        def one_row(row, carry, layer=layer, src=src, dst=dst, last=last):
            def one_group(group, inner):
                lanes8 = pl.ds(pl.multiple_of(group * 8, 8), 8)
                weights = [slabs_ref[27 * layer + tap, lanes8, :] for tap in range(27)]
                running = {}
                for source in range(rounds):
                    cut = pl.ds(source * columns, columns)
                    held = [spread(feats[src, row - 1 + b, lanes8, cut]) for b in range(3)]
                    for a in range(3):
                        t = source - a + 1
                        if t < 0 or t >= rounds:
                            continue
                        for b in range(3):
                            for e in range(3):
                                term = weights[9 * a + 3 * b + e] * held[b][e]
                                running[t] = term if t not in running else running[t] + term
                    done = source - 1 if source < rounds - 1 else None
                    for t in ([done] if done is not None else [rounds - 2, rounds - 1]):
                        if t >= 0:
                            depth[lanes8, pl.ds(t * columns, columns)] = running.pop(t)
                return inner

            lax.fori_loop(0, groups, one_group, 0, unroll=8)
            mixed = jnp.dot(
                mix_ref[layer], depth[...].astype(jnp.bfloat16), preferred_element_type=jnp.float32
            )
            keep = inside(row)
            sums = []
            for t in range(rounds):
                cut = pl.ds(t * columns, columns)
                activated = gelu(mixed[:, t * columns : (t + 1) * columns] + small_ref[3 + layer])
                value = (feats[src, row, :, cut] + activated).astype(jnp.bfloat16).astype(jnp.float32)
                value = jnp.where(keep, value, 0.0)
                if last:
                    sums.append(jnp.sum(value * read_ref[...], axis=0, keepdims=True))
                else:
                    feats[dst, row, :, cut] = value
            if last:
                for t in range(rounds):
                    out_ref[t, pl.ds(row - halo, 1), :] = sums[t]
            return carry

        lax.fori_loop(layer + 1, extended - layer - 1, one_row, 0)


def run_network(planes, embed_gain, embed_bias, depth_kernel, point_weight, point_bias, read_weight, rows, halo):
    span, extended, commit, columns = planes.shape
    rounds = span * commit
    layers, channels, _ = depth_kernel.shape
    lane = jnp.arange(columns)
    side = jnp.arange(27) % 3
    cancel = ((side[:, None] == 0) & (lane == 0)) | ((side[:, None] == 2) & (lane == columns - 1))
    taps = jnp.broadcast_to(jnp.transpose(depth_kernel, (0, 2, 1))[..., None], (layers, 27, channels, columns))
    slabs = jnp.where(cancel[None, :, None, :], 0.0, taps).reshape(layers * 27, channels, columns)
    stacked = jnp.concatenate(
        [embed_gain[None], embed_bias[None], read_weight.astype(jnp.float32)[None], point_bias], axis=0
    )
    small = jnp.broadcast_to(stacked[..., None], stacked.shape + (columns,))
    mix = jnp.transpose(point_weight, (0, 2, 1)).astype(jnp.bfloat16)
    vmem = pl.BlockSpec(memory_space=pltpu.VMEM)
    return pl.pallas_call(
        functools.partial(network_kernel, rows, halo, layers),
        out_shape=jax.ShapeDtypeStruct((rounds, rows, columns), jnp.float32),
        in_specs=[vmem] * 4,
        out_specs=vmem,
        scratch_shapes=[
            pltpu.VMEM((2, extended, channels, rounds * columns), jnp.float32),
            pltpu.VMEM((channels, rounds * columns), jnp.float32),
        ],
        compiler_params=pltpu.CompilerParams(vmem_limit_bytes=56 * 1024 * 1024),
    )(planes, slabs, small, mix)


def shards(
    axis_names,
    syndromes,
    confidence,
    embed_gain,
    embed_bias,
    depth_kernel,
    point_weight,
    point_bias,
    read_weight,
):
    layers = depth_kernel.shape[0]
    rows = syndromes.shape[1]
    signed_slab = ((2 * syndromes - 1).astype(jnp.float32) * confidence).astype(jnp.bfloat16)
    planes = gather_window(signed_slab, layers, axis_names)
    logits = run_network(
        planes, embed_gain, embed_bias, depth_kernel, point_weight, point_bias, read_weight, rows, layers
    )
    return logits[None]


def solution(mesh):
    placed = (P("win", "tile", None), P("win", "tile", None), P(), P(), P(), P(), P(), P())
    return jax.shard_map(
        functools.partial(shards, tuple(mesh.axis_names)), mesh=mesh, in_specs=placed, out_specs=P("win", None, "tile", None), check_vma=False
    )
```

```python
import functools

import jax
import jax.numpy as jnp
from jax import lax
from jax.experimental import pallas as pl
from jax.experimental.pallas import tpu as pltpu
from jax.sharding import PartitionSpec as P

WINDOW = 16
COMMIT = 2


def exchange_kernel(axis_names, halo, slab_ref, out_ref, held, recv_sem, send_sem, local_sem):
    tiles, wins = lax.axis_size("tile"), lax.axis_size("win")
    tile, win = lax.axis_index("tile"), lax.axis_index("win")
    pieces, rows = slab_ref.shape[0], slab_ref.shape[1]
    span = held.shape[0]

    def device(tile_index, win_index):
        place = {"tile": tile_index, "win": win_index}
        return tuple(place[name] for name in axis_names)

    mesh_ids = pl.DeviceIdType.MESH
    blank = jnp.zeros((span, halo) + held.shape[2:], held.dtype)

    @pl.when(tile == 0)
    def _():
        held[:, pl.ds(0, halo)] = blank

    @pl.when(tile == tiles - 1)
    def _():
        held[:, pl.ds(rows + halo, halo)] = blank

    neighbour_tiles = 1 + (tile > 0).astype(jnp.int32) + (tile < tiles - 1).astype(jnp.int32)
    barrier = pltpu.get_barrier_semaphore()
    for shift in (-1, 0, 1):
        for other in range(wins):
            there = tile + shift
            partner = (there >= 0) & (there < tiles)
            if shift == 0:
                partner = partner & (win != other)

            @pl.when(partner)
            def _():
                pl.semaphore_signal(barrier, 1, device_id=device(there, other), device_id_type=mesh_ids)

    pl.semaphore_wait(barrier, neighbour_tiles * wins - 1)

    parts = ((-1, 0, rows + halo, halo, 0), (0, 0, halo, rows, 1), (1, rows - halo, 0, halo, 0))
    started = []
    for piece in range(pieces):
        global_piece = win * pieces + piece
        for other in range(wins):
            offset = global_piece - other
            needed = (offset >= 0) & (offset < span)
            offset = jnp.clip(offset, 0, span - 1)
            for shift, src_row, dst_row, count, kind in parts:
                there = tile + shift
                ok = needed & (there >= 0) & (there < tiles)
                there = jnp.clip(there, 0, tiles - 1)
                src = slab_ref.at[pl.ds(piece, 1), pl.ds(src_row, count)]
                dst = held.at[pl.ds(offset, 1), pl.ds(dst_row, count)]
                if shift == 0:
                    local = ok & (win == other)
                    remote = ok & (win != other)
                    copy_local = pltpu.make_async_copy(src, dst, local_sem)

                    @pl.when(local)
                    def _():
                        copy_local.start()
                        copy_local.wait()
                else:
                    remote = ok
                copy = pltpu.make_async_remote_copy(
                    src_ref=src,
                    dst_ref=dst,
                    send_sem=send_sem.at[piece, other, shift + 1],
                    recv_sem=recv_sem.at[offset, shift + 1],
                    device_id=device(there, other),
                    device_id_type=mesh_ids,
                )

                @pl.when(remote)
                def _():
                    copy.start()

                started.append((remote, copy))

    for remote, copy in started:

        @pl.when(remote)
        def _():
            copy.wait_send()

    for step in range(span):
        source_win = (win + step) // pieces
        for shift, src_row, dst_row, count, kind in parts:
            there = tile - shift
            ok = (there >= 0) & (there < tiles)
            if shift == 0:
                ok = ok & (source_win != win)
            probe = pltpu.make_async_remote_copy(
                src_ref=slab_ref.at[pl.ds(0, 1), pl.ds(src_row, count)],
                dst_ref=held.at[pl.ds(0, 1), pl.ds(dst_row, count)],
                send_sem=send_sem.at[0, 0, shift + 1],
                recv_sem=recv_sem.at[step, shift + 1],
                device_id=device(there, win),
                device_id_type=mesh_ids,
            )

            @pl.when(ok)
            def _():
                probe.wait_recv()

    out_ref[...] = held[...]


def gather_window(signed_slab, halo, axis_names):
    rounds, rows, columns = signed_slab.shape
    pieces = rounds // COMMIT
    span = WINDOW // COMMIT
    cut = jnp.transpose(signed_slab.reshape(pieces, COMMIT, rows, columns), (0, 2, 1, 3))
    shape = (span, rows + 2 * halo, COMMIT, columns)
    held = pl.pallas_call(
        functools.partial(exchange_kernel, axis_names, halo),
        out_shape=jax.ShapeDtypeStruct(shape, signed_slab.dtype),
        in_specs=[pl.BlockSpec(memory_space=pltpu.VMEM)],
        out_specs=pl.BlockSpec(memory_space=pltpu.VMEM),
        scratch_shapes=[
            pltpu.VMEM(shape, signed_slab.dtype),
            pltpu.SemaphoreType.DMA((span, 3)),
            pltpu.SemaphoreType.DMA((pieces, lax.axis_size("win"), 3)),
            pltpu.SemaphoreType.DMA,
        ],
        compiler_params=pltpu.CompilerParams(collective_id=0, has_side_effects=True),
    )(cut)
    return held


def gelu(value):
    half = 0.5 * value
    inner = value * (0.7978845608028654 + 0.035677408136300125 * (value * value))
    return half + half * jnp.tanh(inner)


def network_kernel(rows, halo, layers, planes_ref, slabs_ref, small_ref, mix_ref, out_ref, feats, depth):
    span, extended, commit, columns = planes_ref.shape
    rounds = span * commit
    channels = slabs_ref.shape[1]
    gain_ref, bias_ref, read_ref = small_ref.at[0], small_ref.at[1], small_ref.at[2]
    groups = channels // 8
    tiles = lax.axis_size("tile")
    first_row = lax.axis_index("tile") * rows - halo

    def inside(row):
        plane_row = first_row + row
        return (plane_row >= 0) & (plane_row < rows * tiles)

    def embed(row, carry):
        keep = inside(row)
        for t in range(rounds):
            plane = planes_ref[t // commit, row, pl.ds(t % commit, 1), :].astype(jnp.float32)
            value = plane * gain_ref[...] + bias_ref[...]
            value = value.astype(jnp.bfloat16).astype(jnp.float32)
            feats[0, row, :, pl.ds(t * columns, columns)] = jnp.where(keep, value, 0.0)
        return carry

    lax.fori_loop(0, extended, embed, 0)

    def spread(value):
        return (pltpu.roll(value, 1, 1), value, pltpu.roll(value, columns - 1, 1))

    for layer in range(layers):
        src, dst = layer % 2, (layer + 1) % 2
        last = layer == layers - 1

        def one_row(row, carry, layer=layer, src=src, dst=dst, last=last):
            def one_group(group, inner):
                lanes8 = pl.ds(pl.multiple_of(group * 8, 8), 8)
                weights = [slabs_ref[27 * layer + tap, lanes8, :] for tap in range(27)]
                running = {}
                for source in range(rounds):
                    cut = pl.ds(source * columns, columns)
                    held = [spread(feats[src, row - 1 + b, lanes8, cut]) for b in range(3)]
                    for a in range(3):
                        t = source - a + 1
                        if t < 0 or t >= rounds:
                            continue
                        for b in range(3):
                            for e in range(3):
                                term = weights[9 * a + 3 * b + e] * held[b][e]
                                running[t] = term if t not in running else running[t] + term
                    done = source - 1 if source < rounds - 1 else None
                    for t in ([done] if done is not None else [rounds - 2, rounds - 1]):
                        if t >= 0:
                            depth[lanes8, pl.ds(t * columns, columns)] = running.pop(t)
                return inner

            lax.fori_loop(0, groups, one_group, 0, unroll=8)
            mixed = jnp.dot(
                mix_ref[layer], depth[...].astype(jnp.bfloat16), preferred_element_type=jnp.float32
            )
            keep = inside(row)
            sums = []
            for t in range(rounds):
                cut = pl.ds(t * columns, columns)
                activated = gelu(mixed[:, t * columns : (t + 1) * columns] + small_ref[3 + layer])
                value = (feats[src, row, :, cut] + activated).astype(jnp.bfloat16).astype(jnp.float32)
                if last:
                    value = jnp.where(keep, value, 0.0)
                    sums.append(jnp.sum(value * read_ref[...], axis=0, keepdims=True))
                else:
                    feats[dst, row, :, cut] = value
            if not last:

                @pl.when(jnp.logical_not(keep))
                def _():
                    feats[dst, row] = jnp.zeros(feats.shape[2:], jnp.float32)

            if last:
                for t in range(rounds):
                    out_ref[t, pl.ds(row - halo, 1), :] = sums[t]
            return carry

        lax.fori_loop(layer + 1, extended - layer - 1, one_row, 0)


def run_network(planes, embed_gain, embed_bias, depth_kernel, point_weight, point_bias, read_weight, rows, halo):
    span, extended, commit, columns = planes.shape
    rounds = span * commit
    layers, channels, _ = depth_kernel.shape
    lane = jnp.arange(columns)
    side = jnp.arange(27) % 3
    cancel = ((side[:, None] == 0) & (lane == 0)) | ((side[:, None] == 2) & (lane == columns - 1))
    taps = jnp.broadcast_to(jnp.transpose(depth_kernel, (0, 2, 1))[..., None], (layers, 27, channels, columns))
    slabs = jnp.where(cancel[None, :, None, :], 0.0, taps).reshape(layers * 27, channels, columns)
    stacked = jnp.concatenate(
        [embed_gain[None], embed_bias[None], read_weight.astype(jnp.float32)[None], point_bias], axis=0
    )
    small = jnp.broadcast_to(stacked[..., None], stacked.shape + (columns,))
    mix = jnp.transpose(point_weight, (0, 2, 1)).astype(jnp.bfloat16)
    vmem = pl.BlockSpec(memory_space=pltpu.VMEM)
    return pl.pallas_call(
        functools.partial(network_kernel, rows, halo, layers),
        out_shape=jax.ShapeDtypeStruct((rounds, rows, columns), jnp.float32),
        in_specs=[vmem] * 4,
        out_specs=vmem,
        scratch_shapes=[
            pltpu.VMEM((2, extended, channels, rounds * columns), jnp.float32),
            pltpu.VMEM((channels, rounds * columns), jnp.float32),
        ],
        compiler_params=pltpu.CompilerParams(vmem_limit_bytes=56 * 1024 * 1024),
    )(planes, slabs, small, mix)


def shards(
    axis_names,
    syndromes,
    confidence,
    embed_gain,
    embed_bias,
    depth_kernel,
    point_weight,
    point_bias,
    read_weight,
):
    layers = depth_kernel.shape[0]
    rows = syndromes.shape[1]
    signed_slab = ((2 * syndromes - 1).astype(jnp.float32) * confidence).astype(jnp.bfloat16)
    planes = gather_window(signed_slab, layers, axis_names)
    logits = run_network(
        planes, embed_gain, embed_bias, depth_kernel, point_weight, point_bias, read_weight, rows, layers
    )
    return logits[None]


def solution(mesh):
    placed = (P("win", "tile", None), P("win", "tile", None), P(), P(), P(), P(), P(), P())
    return jax.shard_map(
        functools.partial(shards, tuple(mesh.axis_names)), mesh=mesh, in_specs=placed, out_specs=P("win", None, "tile", None), check_vma=False
    )
```

```python
import functools

import jax
import jax.numpy as jnp
from jax import lax
from jax.experimental import pallas as pl
from jax.experimental.pallas import tpu as pltpu
from jax.sharding import PartitionSpec as P

WINDOW = 16
COMMIT = 2


def exchange_kernel(axis_names, halo, slab_ref, out_ref, held, recv_sem, send_sem, local_sem):
    tiles, wins = lax.axis_size("tile"), lax.axis_size("win")
    tile, win = lax.axis_index("tile"), lax.axis_index("win")
    pieces, rows = slab_ref.shape[0], slab_ref.shape[1]
    span = held.shape[0]

    def device(tile_index, win_index):
        place = {"tile": tile_index, "win": win_index}
        return tuple(place[name] for name in axis_names)

    mesh_ids = pl.DeviceIdType.MESH
    blank = jnp.zeros((span, halo) + held.shape[2:], held.dtype)

    @pl.when(tile == 0)
    def _():
        held[:, pl.ds(0, halo)] = blank

    @pl.when(tile == tiles - 1)
    def _():
        held[:, pl.ds(rows + halo, halo)] = blank

    neighbour_tiles = 1 + (tile > 0).astype(jnp.int32) + (tile < tiles - 1).astype(jnp.int32)
    barrier = pltpu.get_barrier_semaphore()
    for shift in (-1, 0, 1):
        for other in range(wins):
            there = tile + shift
            partner = (there >= 0) & (there < tiles)
            if shift == 0:
                partner = partner & (win != other)

            @pl.when(partner)
            def _():
                pl.semaphore_signal(barrier, 1, device_id=device(there, other), device_id_type=mesh_ids)

    pl.semaphore_wait(barrier, neighbour_tiles * wins - 1)

    parts = ((-1, 0, rows + halo, halo, 0), (0, 0, halo, rows, 1), (1, rows - halo, 0, halo, 0))
    started = []
    for piece in range(pieces):
        global_piece = win * pieces + piece
        for other in range(wins):
            offset = global_piece - other
            needed = (offset >= 0) & (offset < span)
            offset = jnp.clip(offset, 0, span - 1)
            for shift, src_row, dst_row, count, kind in parts:
                there = tile + shift
                ok = needed & (there >= 0) & (there < tiles)
                there = jnp.clip(there, 0, tiles - 1)
                src = slab_ref.at[pl.ds(piece, 1), pl.ds(src_row, count)]
                dst = held.at[pl.ds(offset, 1), pl.ds(dst_row, count)]
                if shift == 0:
                    local = ok & (win == other)
                    remote = ok & (win != other)
                    copy_local = pltpu.make_async_copy(src, dst, local_sem)

                    @pl.when(local)
                    def _():
                        copy_local.start()
                        copy_local.wait()
                else:
                    remote = ok
                copy = pltpu.make_async_remote_copy(
                    src_ref=src,
                    dst_ref=dst,
                    send_sem=send_sem.at[piece, other, shift + 1],
                    recv_sem=recv_sem.at[offset, shift + 1],
                    device_id=device(there, other),
                    device_id_type=mesh_ids,
                )

                @pl.when(remote)
                def _():
                    copy.start()

                started.append((remote, copy))

    for remote, copy in started:

        @pl.when(remote)
        def _():
            copy.wait_send()

    for step in range(span):
        source_win = (win + step) // pieces
        for shift, src_row, dst_row, count, kind in parts:
            there = tile - shift
            ok = (there >= 0) & (there < tiles)
            if shift == 0:
                ok = ok & (source_win != win)
            probe = pltpu.make_async_remote_copy(
                src_ref=slab_ref.at[pl.ds(0, 1), pl.ds(src_row, count)],
                dst_ref=held.at[pl.ds(0, 1), pl.ds(dst_row, count)],
                send_sem=send_sem.at[0, 0, shift + 1],
                recv_sem=recv_sem.at[step, shift + 1],
                device_id=device(there, win),
                device_id_type=mesh_ids,
            )

            @pl.when(ok)
            def _():
                probe.wait_recv()

    out_ref[...] = held[...]


def gather_window(signed_slab, halo, axis_names):
    rounds, rows, columns = signed_slab.shape
    pieces = rounds // COMMIT
    span = WINDOW // COMMIT
    cut = jnp.transpose(signed_slab.reshape(pieces, COMMIT, rows, columns), (0, 2, 1, 3))
    shape = (span, rows + 2 * halo, COMMIT, columns)
    held = pl.pallas_call(
        functools.partial(exchange_kernel, axis_names, halo),
        out_shape=jax.ShapeDtypeStruct(shape, signed_slab.dtype),
        in_specs=[pl.BlockSpec(memory_space=pltpu.VMEM)],
        out_specs=pl.BlockSpec(memory_space=pltpu.VMEM),
        scratch_shapes=[
            pltpu.VMEM(shape, signed_slab.dtype),
            pltpu.SemaphoreType.DMA((span, 3)),
            pltpu.SemaphoreType.DMA((pieces, lax.axis_size("win"), 3)),
            pltpu.SemaphoreType.DMA,
        ],
        compiler_params=pltpu.CompilerParams(collective_id=0, has_side_effects=True),
    )(cut)
    return held


def gelu(value):
    half = 0.5 * value
    inner = value * (0.7978845608028654 + 0.035677408136300125 * (value * value))
    return half + half * jnp.tanh(inner)


def network_kernel(rows, halo, layers, planes_ref, slabs_ref, small_ref, mix_ref, out_ref, feats, depth):
    span, extended, commit, columns = planes_ref.shape
    rounds = span * commit
    channels = slabs_ref.shape[1]
    gain_ref, bias_ref, read_ref = small_ref.at[0], small_ref.at[1], small_ref.at[2]
    groups = channels // 8
    tiles = lax.axis_size("tile")
    first_row = lax.axis_index("tile") * rows - halo

    def inside(row):
        plane_row = first_row + row
        return (plane_row >= 0) & (plane_row < rows * tiles)

    def embed(row, carry):
        keep = inside(row)
        for t in range(rounds):
            plane = planes_ref[t // commit, row, pl.ds(t % commit, 1), :].astype(jnp.float32)
            value = plane * gain_ref[...] + bias_ref[...]
            value = value.astype(jnp.bfloat16).astype(jnp.float32)
            feats[0, row, :, pl.ds(t * columns, columns)] = value

        @pl.when(jnp.logical_not(keep))
        def _():
            feats[0, row] = jnp.zeros(feats.shape[2:], jnp.float32)

        return carry

    lax.fori_loop(0, extended, embed, 0)

    def spread(value):
        return (pltpu.roll(value, 1, 1), value, pltpu.roll(value, columns - 1, 1))

    for layer in range(layers):
        src, dst = layer % 2, (layer + 1) % 2
        last = layer == layers - 1

        def one_row(row, carry, layer=layer, src=src, dst=dst, last=last):
            def one_group(group, inner):
                lanes8 = pl.ds(pl.multiple_of(group * 8, 8), 8)
                weights = [slabs_ref[27 * layer + tap, lanes8, :] for tap in range(27)]
                running = {}
                for source in range(rounds):
                    cut = pl.ds(source * columns, columns)
                    held = [spread(feats[src, row - 1 + b, lanes8, cut]) for b in range(3)]
                    for a in range(3):
                        t = source - a + 1
                        if t < 0 or t >= rounds:
                            continue
                        for b in range(3):
                            for e in range(3):
                                term = weights[9 * a + 3 * b + e] * held[b][e]
                                running[t] = term if t not in running else running[t] + term
                    done = source - 1 if source < rounds - 1 else None
                    for t in ([done] if done is not None else [rounds - 2, rounds - 1]):
                        if t >= 0:
                            depth[lanes8, pl.ds(t * columns, columns)] = running.pop(t)
                return inner

            lax.fori_loop(0, groups, one_group, 0, unroll=8)
            mixed = jnp.dot(
                mix_ref[layer], depth[...].astype(jnp.bfloat16), preferred_element_type=jnp.float32
            )
            keep = inside(row)
            sums = []
            for t in range(rounds):
                cut = pl.ds(t * columns, columns)
                activated = gelu(mixed[:, t * columns : (t + 1) * columns] + small_ref[3 + layer])
                value = (feats[src, row, :, cut] + activated).astype(jnp.bfloat16).astype(jnp.float32)
                if last:
                    value = jnp.where(keep, value, 0.0)
                    sums.append(jnp.sum(value * read_ref[...], axis=0, keepdims=True))
                else:
                    feats[dst, row, :, cut] = value
            if not last:

                @pl.when(jnp.logical_not(keep))
                def _():
                    feats[dst, row] = jnp.zeros(feats.shape[2:], jnp.float32)

            if last:
                for t in range(rounds):
                    out_ref[t, pl.ds(row - halo, 1), :] = sums[t]
            return carry

        lax.fori_loop(layer + 1, extended - layer - 1, one_row, 0)


def run_network(planes, embed_gain, embed_bias, depth_kernel, point_weight, point_bias, read_weight, rows, halo):
    span, extended, commit, columns = planes.shape
    rounds = span * commit
    layers, channels, _ = depth_kernel.shape
    lane = jnp.arange(columns)
    side = jnp.arange(27) % 3
    cancel = ((side[:, None] == 0) & (lane == 0)) | ((side[:, None] == 2) & (lane == columns - 1))
    taps = jnp.broadcast_to(jnp.transpose(depth_kernel, (0, 2, 1))[..., None], (layers, 27, channels, columns))
    slabs = jnp.where(cancel[None, :, None, :], 0.0, taps).reshape(layers * 27, channels, columns)
    stacked = jnp.concatenate(
        [embed_gain[None], embed_bias[None], read_weight.astype(jnp.float32)[None], point_bias], axis=0
    )
    small = jnp.broadcast_to(stacked[..., None], stacked.shape + (columns,))
    mix = jnp.transpose(point_weight, (0, 2, 1)).astype(jnp.bfloat16)
    vmem = pl.BlockSpec(memory_space=pltpu.VMEM)
    return pl.pallas_call(
        functools.partial(network_kernel, rows, halo, layers),
        out_shape=jax.ShapeDtypeStruct((rounds, rows, columns), jnp.float32),
        in_specs=[vmem] * 4,
        out_specs=vmem,
        scratch_shapes=[
            pltpu.VMEM((2, extended, channels, rounds * columns), jnp.float32),
            pltpu.VMEM((channels, rounds * columns), jnp.float32),
        ],
        compiler_params=pltpu.CompilerParams(vmem_limit_bytes=56 * 1024 * 1024),
    )(planes, slabs, small, mix)


def shards(
    axis_names,
    syndromes,
    confidence,
    embed_gain,
    embed_bias,
    depth_kernel,
    point_weight,
    point_bias,
    read_weight,
):
    layers = depth_kernel.shape[0]
    rows = syndromes.shape[1]
    signed_slab = ((2 * syndromes - 1).astype(jnp.float32) * confidence).astype(jnp.bfloat16)
    planes = gather_window(signed_slab, layers, axis_names)
    logits = run_network(
        planes, embed_gain, embed_bias, depth_kernel, point_weight, point_bias, read_weight, rows, layers
    )
    return logits[None]


def solution(mesh):
    placed = (P("win", "tile", None), P("win", "tile", None), P(), P(), P(), P(), P(), P())
    return jax.shard_map(
        functools.partial(shards, tuple(mesh.axis_names)), mesh=mesh, in_specs=placed, out_specs=P("win", None, "tile", None), check_vma=False
    )
```
